32 devices in a mesh: row: 4 (over y, x), col: 8 (over z, core).
Axes of the slice: x: 2, y: 2, z: 4, core: 2. Of those that a mesh axis runs over, the one named last changes fastest.
Arguments:
- tokens_in: bfloat16 [192, 8192], P('col', 'row'), may hold values from -6 to 6
- grad_out: bfloat16 [192, 8192], P('col', 'row'), may hold values from -6 to 6
- gate_weight: bfloat16 [8192, 28672], P('row', 'col'), may hold values from -0.09375 to 0.09375
- up_weight: bfloat16 [8192, 28672], P('row', 'col'), may hold values from -0.09375 to 0.09375
- down_weight: bfloat16 [28672, 8192], P('col', 'row'), may hold values from -0.046875 to 0.046875
- gate_mask: int32 [128, 448], P('row', 'col'), may hold values 0 or 1
- up_mask: int32 [128, 448], P('row', 'col'), may hold values 0 or 1
- down_mask: int32 [448, 128], P('col', 'row'), may hold values 0 or 1
Outputs:
- layer_out: bfloat16 [192, 8192], P('col', 'row')
- grad_in: bfloat16 [192, 8192], P('col', 'row')
- grad_gate: bfloat16 [8192, 28672], P('row', 'col')
- grad_up: bfloat16 [8192, 28672], P('row', 'col')
- grad_down: bfloat16 [28672, 8192], P('col', 'row')
The draws below stay inside these ranges and needn't reach their ends.
Inputs may be any that keep to these rules, and one draw needn't show every extreme that they name: gate_mask holds only 0 and 1. up_mask holds only 0 and 1. down_mask holds only 0 and 1.
All inputs are finite; a program needn't handle non-finite values. No bound on the sum of `gate_mask` or of `up_mask` or of `down_mask` on one device may be relied on, other than what follows from the above.
Results may differ from the reference program's by a relative error of at most 0.0051.
Values may be sent and summed in bfloat16 or wider, within the bound.
No kernel may reach another device: no remote copies, remote signals or barrier semaphores. Data moves between devices by JAX's collectives and lax.ppermute only.
A program may use at most 448 MiB of HBM per device.

```python
import jax
import jax.numpy as jnp
from jax import lax

D = 8192
FF = 28672
BLOCK = 64
TOKENS = 192


def touch_ends(values, key, least, top_value):
    place = [jax.random.randint(jax.random.fold_in(key, axis), (), 0, length) for axis, length in enumerate(values.shape)]
    widest = values.shape.index(max(values.shape))
    beside = place[:widest] + [(place[widest] + 1) % values.shape[widest]] + place[widest + 1:]
    return values.at[tuple(place)].set(least).at[tuple(beside)].set(top_value)


def shard_levels(stream_key, dims, pieces, low, top_value):
    level, own = 1.0, jax.random.fold_in(stream_key, 6)
    for dim, shards_of in pieces:
        heights = jnp.exp(jax.random.uniform(jax.random.fold_in(own, dim), (shards_of,), jnp.float32, low / len(pieces), top_value / len(pieces)))
        level = level * jnp.repeat(heights, dims[dim] // shards_of).reshape([-1 if axis == dim else 1 for axis in range(len(dims))])
    return level


def bell_draw(rng, extent, deviation, reach, cuts=(), kind=jnp.bfloat16):
    array = deviation * jax.random.normal(rng, extent, jnp.float32)
    if cuts:
        array = array * shard_levels(rng, extent, cuts, -0.22, 0.18)
    return jnp.clip(array, -reach, reach).astype(kind)


def setup_inputs(seed: int = 0) -> dict:
    key_of = jax.random.split(jax.random.key(seed), 9)
    return {
        "tokens_in": bell_draw(key_of[0], (TOKENS, D), 1.0, 6.0, ((0, 8), (1, 4))),
        "grad_out": bell_draw(key_of[1], (TOKENS, D), 1.0, 6.0, ((0, 8), (1, 4))),
        "gate_weight": bell_draw(key_of[2], (D, FF), (D // 2) ** -0.5, 0.09375, ((0, 4), (1, 8))),
        "up_weight": bell_draw(key_of[3], (D, FF), (D // 2) ** -0.5, 0.09375, ((0, 4), (1, 8))),
        "down_weight": bell_draw(key_of[4], (FF, D), (FF // 2) ** -0.5, 0.046875, ((0, 8), (1, 4))),
        "gate_mask": touch_ends((jax.random.randint(key_of[5], (D // BLOCK, FF // BLOCK), 0, 2) < 1).astype(jnp.int32), jax.random.fold_in(key_of[5], 1), 0, 1),
        "up_mask": touch_ends((jax.random.randint(key_of[6], (D // BLOCK, FF // BLOCK), 0, 2) < 1).astype(jnp.int32), jax.random.fold_in(key_of[6], 1), 0, 1),
        "down_mask": touch_ends((jax.random.randint(key_of[7], (FF // BLOCK, D // BLOCK), 0, 2) < 1).astype(jnp.int32), jax.random.fold_in(key_of[7], 1), 0, 1),
    }


def expand_blocks(weight, blocks):
    rows_blk, cols_blk = blocks.shape
    height, width = weight.shape
    shaped = weight.reshape(rows_blk, height // rows_blk, cols_blk, width // cols_blk)
    return (shaped * blocks.astype(weight.dtype)[:, None, :, None]).reshape(height, width)


def contract(left_side, right_side, left_dim, right_dim):
    return lax.dot_general(left_side, right_side, (((left_dim,), (right_dim,)), ((), ())), preferred_element_type=jnp.float32)


def reference(tokens_in, grad_out, gate_weight, up_weight, down_weight, gate_mask, up_mask, down_mask):
    gate_kept = expand_blocks(gate_weight, gate_mask)
    up_kept = expand_blocks(up_weight, up_mask)
    down_kept = expand_blocks(down_weight, down_mask)
    gate_pre = jnp.dot(tokens_in, gate_kept, preferred_element_type=jnp.float32)
    up_pre = jnp.dot(tokens_in, up_kept, preferred_element_type=jnp.float32)
    sig_gate = jax.nn.sigmoid(gate_pre)
    silu_gate = gate_pre * sig_gate
    hidden = (silu_gate * up_pre).astype(jnp.bfloat16)
    layer_out = jnp.dot(hidden, down_kept, preferred_element_type=jnp.float32).astype(jnp.bfloat16)
    grad_hidden = contract(grad_out, down_kept, 1, 1)
    grad_down = expand_blocks(contract(hidden, grad_out, 0, 0), down_mask).astype(jnp.bfloat16)
    grad_gate_pre = (grad_hidden * up_pre * sig_gate * (1.0 + gate_pre * (1.0 - sig_gate))).astype(jnp.bfloat16)
    grad_up_pre = (grad_hidden * silu_gate).astype(jnp.bfloat16)
    grad_in = (contract(grad_gate_pre, gate_kept, 1, 1) + contract(grad_up_pre, up_kept, 1, 1)).astype(jnp.bfloat16)
    grad_gate = expand_blocks(contract(tokens_in, grad_gate_pre, 0, 0), gate_mask).astype(jnp.bfloat16)
    grad_up = expand_blocks(contract(tokens_in, grad_up_pre, 0, 0), up_mask).astype(jnp.bfloat16)
    return (layer_out, grad_in, grad_gate, grad_up, grad_down)
```

```python
import functools

import jax
import jax.numpy as jnp
from jax import lax
from jax.experimental import pallas as pl
from jax.experimental.pallas import tpu as pltpu
from jax.sharding import PartitionSpec as P

BF16 = jnp.bfloat16
F32 = jnp.float32
VMEM_LIMIT = 56 * 1024 * 1024
NT = (((1,), (1,)), ((), ()))


def dot(a, b):
    return jnp.dot(a, b, preferred_element_type=F32)


def spread(mask, first, width, block):
    count = mask.shape[-1]
    col = lax.broadcasted_iota(jnp.int32, (count, width), 1) // block + first
    row = lax.broadcasted_iota(jnp.int32, (count, width), 0)
    return dot(mask.astype(BF16), jnp.where(row == col, 1.0, 0.0).astype(BF16))


def masked_tile(w_ref, spread_mask, out_ref, block):
    width = w_ref.shape[1]
    for i in range(w_ref.shape[0] // block):
        keep = jnp.broadcast_to(spread_mask[i : i + 1, :], (block, width)).astype(BF16)
        out_ref[i * block : (i + 1) * block, :] = w_ref[i * block : (i + 1) * block, :] * keep


def load_quarters(refs, scratch):
    quarter = scratch.shape[0] // 4

    @pl.when(pl.program_id(0) == 0)
    def _():
        for j, ref in enumerate(refs):
            scratch[j * quarter : (j + 1) * quarter, :] = ref[0]


def quarter_specs(rows, width):
    return [
        pl.BlockSpec((1, rows, width), functools.partial(lambda i, me, j: (me[0] ^ j, 0, 0), j=j))
        for j in range(4)
    ]


def put_halves(part, send, keep, x_first):
    quarter = part.shape[0] // 4
    kept, sent = ((0, 2), (1, 3)) if x_first else ((0, 1), (2, 3))
    for slot in range(2):
        rows = slice(slot * quarter, (slot + 1) * quarter)
        keep[rows, :] = part[kept[slot] * quarter : (kept[slot] + 1) * quarter, :]
        send[rows, :] = part[sent[slot] * quarter : (sent[slot] + 1) * quarter, :].astype(BF16)


def join_halves(first, second, x_first):
    quarter = first.shape[0] // 2
    if not x_first:
        return jnp.concatenate([first[...], second[...]], axis=0)
    return jnp.concatenate(
        [first[:quarter, :], second[:quarter, :], first[quarter:, :], second[quarter:, :]], axis=0
    )


def params():
    return pltpu.CompilerParams(
        dimension_semantics=("arbitrary",), vmem_limit_bytes=VMEM_LIMIT
    )


def forward_part(me, tokens, weight, mask, tile, x_first):
    total, depth = tokens.shape
    quarter = total // 4
    width = weight.shape[1]
    block = depth // mask.shape[0]

    def body(me_ref, q0, q1, q2, q3, w_ref, m_ref, send, keep, x_s, w_s):
        load_quarters((q0, q1, q2, q3), x_s)
        m = spread(m_ref[...], pl.program_id(0) * (tile // block), tile, block)
        masked_tile(w_ref, m, w_s, block)
        put_halves(dot(x_s[...], w_s[...]), send, keep, x_first)

    split = tokens.reshape(4, quarter, depth)
    return pl.pallas_call(
        body,
        grid_spec=pltpu.PrefetchScalarGridSpec(
            num_scalar_prefetch=1,
            grid=(width // tile,),
            in_specs=quarter_specs(quarter, depth)
            + [
                pl.BlockSpec((depth, tile), lambda i, me: (0, i)),
                pl.BlockSpec(mask.shape, lambda i, me: (0, 0)),
            ],
            out_specs=[pl.BlockSpec((total // 2, tile), lambda i, me: (0, i))] * 2,
            scratch_shapes=[pltpu.VMEM((total, depth), BF16), pltpu.VMEM((depth, tile), BF16)],
        ),
        out_shape=[
            jax.ShapeDtypeStruct((total // 2, width), BF16),
            jax.ShapeDtypeStruct((total // 2, width), F32),
        ],
        compiler_params=params(),
        cost_estimate=pl.CostEstimate(
            flops=2 * total * depth * width,
            bytes_accessed=2 * depth * width + 3 * total * width,
            transcendentals=0,
        ),
        name="forward_part",
    )(me, split, split, split, split, weight, mask)


def hidden_part(me, grads, weight, mask, tile, first, steps, x_first):
    total, depth = grads.shape
    quarter = total // 4
    per = mask.shape[1]
    block = tile // per

    def body(me_ref, q0, q1, q2, q3, w_ref, m_ref, send, keep, x_s, w_s):
        load_quarters((q0, q1, q2, q3), x_s)
        m = spread(m_ref[0], 0, depth, block)
        masked_tile(w_ref, m, w_s, block)
        part = lax.dot_general(x_s[...], w_s[...], NT, preferred_element_type=F32)
        put_halves(part, send, keep, x_first)

    split = grads.reshape(4, quarter, depth)
    return pl.pallas_call(
        body,
        grid_spec=pltpu.PrefetchScalarGridSpec(
            num_scalar_prefetch=1,
            grid=(steps,),
            in_specs=quarter_specs(quarter, depth)
            + [
                pl.BlockSpec((tile, depth), lambda i, me: (i + first, 0)),
                pl.BlockSpec((1,) + mask.shape[1:], lambda i, me: (i + first, 0, 0)),
            ],
            out_specs=[pl.BlockSpec((total // 2, tile), lambda i, me: (0, i))] * 2,
            scratch_shapes=[pltpu.VMEM((total, depth), BF16), pltpu.VMEM((tile, depth), BF16)],
        ),
        out_shape=[
            jax.ShapeDtypeStruct((total // 2, steps * tile), BF16),
            jax.ShapeDtypeStruct((total // 2, steps * tile), F32),
        ],
        compiler_params=params(),
        cost_estimate=pl.CostEstimate(
            flops=2 * total * depth * steps * tile,
            bytes_accessed=2 * depth * steps * tile + 3 * total * steps * tile,
            transcendentals=0,
        ),
        name="hidden_part",
    )(me, split, split, split, split, weight, mask)


def put_owners(place, total, send, keep, owners):
    rows = total.shape[0] // owners
    per = owners // 4
    bits = owners.bit_length() - 1
    me, col = place[0], place[1]
    half = owners // 2
    for pair in range(owners // 2):
        pieces = []
        for spot in (2 * pair, 2 * pair + 1):
            step = sum(((spot >> b) & 1) << (bits - 1 - b) for b in range(bits))
            owner = col ^ step
            start = (((owner // per) ^ me) * per + owner % per) * rows
            pieces.append(total[pl.ds(pl.multiple_of(start, 8), rows), :])
        both = jnp.concatenate(pieces, axis=0)
        if pair < half // 2:
            keep[2 * pair * rows : (2 * pair + 2) * rows, :] = both
        else:
            at = 2 * pair - half
            send[at * rows : (at + 2) * rows, :] = both


def down_back(place, first_half, second_half, grads, weight, mask, tile, owners, x_first):
    total, depth = grads.shape
    quarter = total // 4
    width = weight.shape[0]
    per = mask.shape[1]
    block = tile // per

    def body(place_ref, q0, q1, q2, q3, h0, h1, w_ref, m_ref, gw, send, keep, g_s, w_s, acc):
        load_quarters((q0, q1, q2, q3), g_s)
        step = pl.program_id(0)
        m = spread(m_ref[0], 0, depth, block)
        masked_tile(w_ref, m, w_s, block)
        hid = join_halves(h0, h1, x_first)
        out = dot(hid, w_s[...])

        @pl.when(step == 0)
        def _():
            acc[...] = out

        @pl.when(step != 0)
        def _():
            acc[...] += out

        hid_t = hid.T
        for i in range(per):
            rows = slice(i * block, (i + 1) * block)
            gw[rows, :] = (dot(hid_t[rows, :], g_s[...]) * m[i : i + 1, :]).astype(BF16)

        @pl.when(step == pl.num_programs(0) - 1)
        def _():
            put_owners(place_ref, acc, send, keep, owners)

    split = grads.reshape(4, quarter, depth)
    return pl.pallas_call(
        body,
        grid_spec=pltpu.PrefetchScalarGridSpec(
            num_scalar_prefetch=1,
            grid=(width // tile,),
            in_specs=quarter_specs(quarter, depth)
            + [pl.BlockSpec((total // 2, tile), lambda i, me: (0, i))] * 2
            + [
                pl.BlockSpec((tile, depth), lambda i, me: (i, 0)),
                pl.BlockSpec((1,) + mask.shape[1:], lambda i, me: (i, 0, 0)),
            ],
            out_specs=[pl.BlockSpec((tile, depth), lambda i, me: (i, 0))]
            + [pl.BlockSpec((total // 2, depth), lambda i, me: (0, 0))] * 2,
            scratch_shapes=[
                pltpu.VMEM((total, depth), BF16),
                pltpu.VMEM((tile, depth), BF16),
                pltpu.VMEM((total, depth), F32),
            ],
        ),
        out_shape=[
            jax.ShapeDtypeStruct((width, depth), BF16),
            jax.ShapeDtypeStruct((total // 2, depth), F32),
            jax.ShapeDtypeStruct((total // 2, depth), F32),
        ],
        compiler_params=params(),
        cost_estimate=pl.CostEstimate(
            flops=4 * total * depth * width,
            bytes_accessed=4 * depth * width,
            transcendentals=0,
        ),
        name="down_back",
    )(place, split, split, split, split, first_half, second_half, weight, mask)


def input_back(place, gate_halves, up_halves, gate_w, up_w, gate_m, up_m, tile, owners):
    depth, width = gate_w.shape
    total = 2 * gate_halves[0].shape[0]
    block = depth // gate_m.shape[0]

    def body(place_ref, a0, a1, b0, b1, gw_ref, uw_ref, gm, um, send, keep, g_s, u_s, acc):
        step = pl.program_id(0)
        first = step * (tile // block)
        masked_tile(gw_ref, spread(gm[...], first, tile, block), g_s, block)
        masked_tile(uw_ref, spread(um[...], first, tile, block), u_s, block)
        out = lax.dot_general(
            join_halves(a0, a1, True), g_s[...], NT, preferred_element_type=F32
        ) + lax.dot_general(join_halves(b0, b1, False), u_s[...], NT, preferred_element_type=F32)

        @pl.when(step == 0)
        def _():
            acc[...] = out

        @pl.when(step != 0)
        def _():
            acc[...] += out

        @pl.when(step == pl.num_programs(0) - 1)
        def _():
            put_owners(place_ref, acc, send, keep, owners)

    return pl.pallas_call(
        body,
        grid_spec=pltpu.PrefetchScalarGridSpec(
            num_scalar_prefetch=1,
            grid=(width // tile,),
            in_specs=[pl.BlockSpec((total // 2, tile), lambda i, me: (0, i))] * 4
            + [pl.BlockSpec((depth, tile), lambda i, me: (0, i))] * 2
            + [pl.BlockSpec(gate_m.shape, lambda i, me: (0, 0))] * 2,
            out_specs=[pl.BlockSpec((total // 2, depth), lambda i, me: (0, 0))] * 2,
            scratch_shapes=[
                pltpu.VMEM((depth, tile), BF16),
                pltpu.VMEM((depth, tile), BF16),
                pltpu.VMEM((total, depth), F32),
            ],
        ),
        out_shape=[
            jax.ShapeDtypeStruct((total // 2, depth), F32),
            jax.ShapeDtypeStruct((total // 2, depth), F32),
        ],
        compiler_params=params(),
        cost_estimate=pl.CostEstimate(
            flops=4 * total * depth * width,
            bytes_accessed=4 * depth * width,
            transcendentals=0,
        ),
        name="input_back",
    )(place, *gate_halves, *up_halves, gate_w, up_w, gate_m, up_m)


def weight_back(me, gate_halves, up_halves, tokens, gate_m, up_m, tile):
    total, depth = tokens.shape
    quarter = total // 4
    width = gate_halves[0].shape[1]
    block = depth // gate_m.shape[0]
    rows_at_once = min(256, depth)

    def body(me_ref, q0, q1, q2, q3, a0, a1, b0, b1, gm, um, gg, gu, x_t):
        @pl.when(pl.program_id(0) == 0)
        def _():
            x_t[...] = jnp.concatenate([q0[0], q1[0], q2[0], q3[0]], axis=0).T

        first = pl.program_id(0) * (tile // block)
        for pre, mask, out in (
            (join_halves(a0, a1, True), gm, gg),
            (join_halves(b0, b1, False), um, gu),
        ):
            m = spread(mask[...], first, tile, block)
            for top in range(0, depth, rows_at_once):
                got = dot(x_t[top : top + rows_at_once, :], pre)
                for i in range(rows_at_once // block):
                    line = top // block + i
                    out[top + i * block : top + (i + 1) * block, :] = (
                        got[i * block : (i + 1) * block, :] * m[line : line + 1, :]
                    ).astype(BF16)

    split = tokens.reshape(4, quarter, depth)
    return pl.pallas_call(
        body,
        grid_spec=pltpu.PrefetchScalarGridSpec(
            num_scalar_prefetch=1,
            grid=(width // tile,),
            in_specs=quarter_specs(quarter, depth)
            + [pl.BlockSpec((total // 2, tile), lambda i, me: (0, i))] * 4
            + [pl.BlockSpec(gate_m.shape, lambda i, me: (0, 0))] * 2,
            out_specs=[pl.BlockSpec((depth, tile), lambda i, me: (0, i))] * 2,
            scratch_shapes=[pltpu.VMEM((depth, total), BF16)],
        ),
        out_shape=[jax.ShapeDtypeStruct((depth, width), BF16)] * 2,
        compiler_params=params(),
        cost_estimate=pl.CostEstimate(
            flops=4 * total * depth * width,
            bytes_accessed=4 * depth * width,
            transcendentals=0,
        ),
        name="weight_back",
    )(me, split, split, split, split, *gate_halves, *up_halves, gate_m, up_m)


def swap(value, axis, size, bit):
    return lax.ppermute(value, axis, [(i, i ^ bit) for i in range(size)])


def local(rows, cols, tokens_in, grad_out, gate_w, up_w, down_w, gate_mask, up_mask, down_mask):
    me = lax.axis_index("row").astype(jnp.int32)[None]
    place = jnp.stack([lax.axis_index("row"), lax.axis_index("col")]).astype(jnp.int32)
    width = gate_w.shape[1]
    tile = 256 if width % 256 == 0 else 128
    down_m = down_mask.reshape(width // tile, -1, down_mask.shape[1])

    def over_row(value, bit):
        return swap(value, "row", rows, bit)

    def leave(send, keep, x_first):
        first, second = (1, 2) if x_first else (2, 1)
        half = keep + over_row(send, first)
        quarter = half.shape[0] // 2
        return half[:quarter] + over_row(half[quarter:].astype(BF16), second)

    def collect(own, x_first):
        first, second = (2, 1) if x_first else (1, 2)
        near = jnp.concatenate([own, over_row(own, first)], axis=0)
        return near, over_row(near, second)

    def to_owner(send, keep):
        bit = 1
        while True:
            keep = keep + swap(send, "col", cols, bit)
            bit *= 2
            if bit == cols:
                return keep.astype(BF16)
            half = keep.shape[0] // 2
            keep, send = keep[:half], keep[half:].astype(BF16)

    tokens = lax.all_gather(tokens_in, "col", axis=0, tiled=True)
    gate_send, gate_keep = forward_part(me, tokens, gate_w, gate_mask, tile, True)
    up_send, up_keep = forward_part(me, tokens, up_w, up_mask, tile, False)
    up_send, grad_out = lax.optimization_barrier((up_send, grad_out))
    grads = lax.all_gather(grad_out, "col", axis=0, tiled=True)
    tiles = width // tile
    front = (tiles + 1) // 2
    part_a = hidden_part(me, grads, down_w, down_m, tile, 0, front, True)
    part_b = hidden_part(me, grads, down_w, down_m, tile, front, tiles - front, False)
    gate_pre = leave(gate_send, gate_keep, True)
    up_pre = leave(up_send, up_keep, False)
    sig = jax.nn.sigmoid(gate_pre)
    silu = gate_pre * sig
    hidden = collect((silu * up_pre).astype(BF16), False)
    grad_hidden = jnp.concatenate([leave(*part_a, True), leave(*part_b, False)], axis=1)
    grad_gate_pre = (grad_hidden * up_pre * sig * (1.0 + gate_pre * (1.0 - sig))).astype(BF16)
    grad_up_pre = (grad_hidden * silu).astype(BF16)
    gate_halves = collect(grad_gate_pre, True)
    up_halves = collect(grad_up_pre, False)
    grad_down, out_send, out_keep = down_back(
        place, *hidden, grads, down_w, down_m, tile, cols, False
    )
    in_send, in_keep = input_back(
        place, gate_halves, up_halves, gate_w, up_w, gate_mask, up_mask, tile, cols
    )
    grad_gate, grad_up = weight_back(me, gate_halves, up_halves, tokens, gate_mask, up_mask, tile)
    layer_out = to_owner(out_send, out_keep)
    grad_in = to_owner(in_send, in_keep)
    return (layer_out, grad_in, grad_gate, grad_up, grad_down)


def solution(mesh):
    by_row, by_col = P("row", "col"), P("col", "row")
    return jax.shard_map(
        functools.partial(local, mesh.shape["row"], mesh.shape["col"]),
        mesh=mesh,
        in_specs=(by_col, by_col, by_row, by_row, by_col, by_row, by_row, by_col),
        out_specs=(by_col, by_col, by_row, by_row, by_col),
        check_vma=False,
    )
```

```python
import functools

import jax
import jax.numpy as jnp
from jax import lax
from jax.experimental import pallas as pl
from jax.experimental.pallas import tpu as pltpu
from jax.sharding import PartitionSpec as P

BF16 = jnp.bfloat16
F32 = jnp.float32
VMEM_LIMIT = 56 * 1024 * 1024
NT = (((1,), (1,)), ((), ()))
COST = pl.CostEstimate(flops=1000, bytes_accessed=1000, transcendentals=0)


def dot(a, b):
    return jnp.dot(a, b, preferred_element_type=F32)


def spread(mask, block):
    count = mask.shape[1]
    shape = (count, count * block)
    col = lax.broadcasted_iota(jnp.int32, shape, 1) // block
    row = lax.broadcasted_iota(jnp.int32, shape, 0)
    return dot(mask.astype(BF16), jnp.where(row == col, 1.0, 0.0).astype(BF16))


def masked(w, m, block):
    return jnp.concatenate(
        [
            w[i * block : (i + 1) * block, :]
            * jnp.broadcast_to(m[i : i + 1, :], (block, w.shape[1])).astype(BF16)
            for i in range(w.shape[0] // block)
        ],
        axis=0,
    )


def masked_product(left, right, m, out, block):
    height = left.shape[0]
    some = 256 if height % 256 == 0 else 128
    for top in range(0, height, some):
        got = dot(left[top : top + some, :], right)
        for i in range(some // block):
            line = top // block + i
            out[top + i * block : top + (i + 1) * block, :] = (
                got[i * block : (i + 1) * block, :] * m[line : line + 1, :]
            ).astype(BF16)


def fetches(pairs, columns, size):
    def copy(pair, i):
        source, held, sems = pair
        at = slice(i * size, (i + 1) * size)
        return pltpu.make_async_copy(
            source.at[:, at] if columns else source.at[at, :], held.at[i], sems.at[i]
        )

    def begin():
        for i in range(pairs[0][1].shape[0]):
            for pair in pairs:
                copy(pair, i).start()

    def arrived(i):
        for pair in pairs:
            copy(pair, i).wait()

    return begin, arrived


def at_step(pairs, columns, size, prepare):
    begin, arrived = fetches(pairs, columns, size)
    step = pl.program_id(0)

    @pl.when(step == 0)
    def _():
        begin()
        prepare()

    for i in range(pairs[0][1].shape[0]):
        pl.when(step == i)(functools.partial(arrived, i))
    return step


def spread_steps(mask, block, columns, out):
    full = spread(mask, block)
    steps, height, width = out.shape
    for i in range(steps):
        if columns:
            out[i] = full[:, i * width : (i + 1) * width]
        else:
            out[i] = full[i * height : (i + 1) * height, :]


def order_by_row(me, source, out):
    quarter = out.shape[0] // 4
    for j in range(4):
        at = pl.ds(pl.multiple_of((me ^ j) * quarter, 16), quarter)
        out[j * quarter : (j + 1) * quarter, :] = source[at, :]


def join_halves(me, pieces, out):
    quarter = out.shape[0] // 4
    left = 0
    for x_first, near, far in pieces:
        at = slice(left, left + near.shape[1])
        left += near.shape[1]
        for half, spots in (
            (near, (0, 2) if x_first else (0, 1)),
            (far, (1, 3) if x_first else (2, 3)),
        ):
            for slot, j in enumerate(spots):
                rows = pl.ds(pl.multiple_of((me ^ j) * quarter, 16), quarter)
                out[rows, at] = half[slot * quarter : (slot + 1) * quarter, :]


def put_halves(part, send, keep, at, x_first):
    quarter = part.shape[0] // 4
    kept, sent = ((0, 2), (1, 3)) if x_first else ((0, 1), (2, 3))
    for slot in range(2):
        rows = slice(slot * quarter, (slot + 1) * quarter)
        keep[rows, at] = part[kept[slot] * quarter : (kept[slot] + 1) * quarter, :]
        send[rows, at] = part[sent[slot] * quarter : (sent[slot] + 1) * quarter, :].astype(BF16)


def call(body, name, inputs, kinds, outs, out_kinds, scratch, steps=None, maps=None, aliases={}):
    spec = {
        "s": pl.BlockSpec(memory_space=pltpu.SMEM),
        "v": pl.BlockSpec(memory_space=pltpu.VMEM),
        "h": pl.BlockSpec(memory_space=pl.ANY),
    }
    out_specs = [spec[kind] for kind in out_kinds] if maps is None else maps
    grid = {} if steps is None else {"grid": (steps,)}
    return pl.pallas_call(
        body,
        in_specs=[spec[kind] for kind in kinds],
        out_specs=out_specs,
        out_shape=outs,
        scratch_shapes=scratch,
        input_output_aliases=aliases,
        compiler_params=pltpu.CompilerParams(vmem_limit_bytes=VMEM_LIMIT),
        cost_estimate=COST,
        name=name,
        **grid,
    )(*inputs)


def tiles_of(count, height, width):
    return [pltpu.VMEM((count, height, width), BF16), pltpu.SemaphoreType.DMA((count,))]


def shaped(*shape, kind=F32):
    return jax.ShapeDtypeStruct(shape, kind)


def parts_of(tile):
    some = min(tile, 256)
    return [slice(left, left + some) for left in range(0, tile, some)]


def forward_part(me, tokens, weight, mask, tile, x_first):
    total, depth = tokens.shape
    width = weight.shape[1]
    steps = width // tile
    block = depth // mask.shape[0]

    def body(me_ref, x_ref, w_hbm, m_ref, send, keep, x_s, m_s, held, sems):
        def prepare():
            order_by_row(me_ref[0], x_ref, x_s)
            spread_steps(m_ref[...], block, True, m_s)

        step = at_step([(w_hbm, held, sems)], True, tile, prepare)
        w, m = held.at[step], m_s[step]
        for at in parts_of(tile):
            part = dot(x_s[...], masked(w.at[:, at], m[:, at], block))
            put_halves(part, send, keep, at, x_first)

    return call(
        body,
        "forward_part",
        (me, tokens, weight, mask),
        "svhv",
        [shaped(total // 2, width, kind=BF16), shaped(total // 2, width)],
        None,
        [
            pltpu.VMEM((total, depth), BF16),
            pltpu.VMEM((steps, mask.shape[0], tile), F32),
            *tiles_of(steps, depth, tile),
        ],
        steps,
        [pl.BlockSpec((total // 2, tile), lambda i: (0, i))] * 2,
    )


def hidden_part(me, grads, weight, mask, tile):
    total, depth = grads.shape
    steps = weight.shape[0] // tile
    front = (steps + 1) // 2
    block = depth // mask.shape[1]
    per = tile // block

    def body(me_ref, x_ref, w_hbm, m_ref, a_send, a_keep, b_send, b_keep, x_s, m_s, held, sems):
        def prepare():
            order_by_row(me_ref[0], x_ref, x_s)
            spread_steps(m_ref[...], block, False, m_s)

        step = at_step([(w_hbm, held, sems)], False, tile, prepare)
        w, m = held.at[step], m_s[step]

        def put(send, keep, x_first):
            for at in parts_of(tile):
                rows = slice(at.start // block, at.stop // block)
                part = lax.dot_general(
                    x_s[...], masked(w.at[at, :], m[rows, :], block), NT, preferred_element_type=F32
                )
                put_halves(part, send, keep, at, x_first)

        pl.when(step < front)(functools.partial(put, a_send, a_keep, True))
        pl.when(step >= front)(functools.partial(put, b_send, b_keep, False))

    return call(
        body,
        "hidden_part",
        (me, grads, weight, mask),
        "svhv",
        [
            shaped(total // 2, count * tile, kind=kind)
            for count in (front, steps - front)
            for kind in (BF16, F32)
        ],
        None,
        [
            pltpu.VMEM((total, depth), BF16),
            pltpu.VMEM((steps, per, depth), F32),
            *tiles_of(steps, tile, depth),
        ],
        steps,
        [pl.BlockSpec((total // 2, tile), lambda i: (0, jnp.minimum(i, front - 1)))] * 2
        + [pl.BlockSpec((total // 2, tile), lambda i: (0, jnp.maximum(i - front, 0)))] * 2,
    )


def down_back(me, pieces, grads, weight, mask, tile):
    total, depth = grads.shape
    width = weight.shape[0]
    block = width // mask.shape[0]
    steps, slots = depth // tile, 4

    def body(me_ref, h0, h1, h2, h3, g_ref, w_hbm, m_ref, gw, send, keep, hid, hid_t, held, sems, stage, outs):
        begin, arrived = fetches([(w_hbm, held, sems)], True, tile)
        begin()
        join_halves(me_ref[0], ((True, h0, h1), (False, h2, h3)), hid)
        hid_t[...] = hid[...].T
        m = spread(m_ref[...], block)

        def leave(i):
            at = slice(i * tile, (i + 1) * tile)
            return pltpu.make_async_copy(stage.at[i % slots], gw.at[:, at], outs.at[i % slots])

        arrived(0)
        w = masked(held.at[0], m[:, :tile], block)
        for i in range(steps):
            at = slice(i * tile, (i + 1) * tile)
            now = w
            if i >= slots:
                leave(i - slots).wait()
            if i + 1 < steps:
                arrived(i + 1)
                w = masked(held.at[i + 1], m[:, (i + 1) * tile : (i + 2) * tile], block)
            out = dot(hid[...], now)
            keep[:, at] = out[: total // 2, :]
            send[:, at] = out[total // 2 :, :]
            masked_product(hid_t, g_ref[:, at], m[:, at], stage.at[i % slots], block)
            leave(i).start()
        for i in range(max(steps - slots, 0), steps):
            leave(i).wait()

    return call(
        body,
        "down_back",
        (me, *pieces, grads, weight, mask),
        "svvvvvhv",
        [shaped(width, depth, kind=BF16), shaped(total // 2, depth), shaped(total // 2, depth)],
        "hvv",
        [
            pltpu.VMEM((total, width), BF16),
            pltpu.VMEM((width, total), BF16),
            *tiles_of(steps, width, tile),
            pltpu.VMEM((slots, width, tile), BF16),
            pltpu.SemaphoreType.DMA((slots,)),
        ],
    )


def input_back(me, gate_pieces, up_pieces, gate_w, up_w, gate_m, up_m, tile):
    depth, width = gate_w.shape
    total = 2 * gate_pieces[0].shape[0]
    block = depth // gate_m.shape[0]
    steps, per = depth // tile, tile // block

    def body(me_ref, *refs):
        pieces, (gw, uw, gm, um, send, keep, a_s, b_s, gm_s, um_s, gh, gs, uh, us) = refs[:8], refs[8:]

        def prepare():
            join_halves(me_ref[0], ((True, *pieces[0:2]), (False, *pieces[2:4])), a_s)
            join_halves(me_ref[0], ((True, *pieces[4:6]), (False, *pieces[6:8])), b_s)
            spread_steps(gm[...], block, False, gm_s)
            spread_steps(um[...], block, False, um_s)

        step = at_step([(gw, gh, gs), (uw, uh, us)], False, tile, prepare)
        out = lax.dot_general(
            a_s[...], masked(gh.at[step], gm_s[step], block), NT, preferred_element_type=F32
        )
        out += lax.dot_general(
            b_s[...], masked(uh.at[step], um_s[step], block), NT, preferred_element_type=F32
        )
        keep[...] = out[: total // 2, :]
        send[...] = out[total // 2 :, :]

    return call(
        body,
        "input_back",
        (me, *gate_pieces, *up_pieces, gate_w, up_w, gate_m, up_m),
        "s" + "v" * 8 + "hhvv",
        [shaped(total // 2, depth), shaped(total // 2, depth)],
        None,
        [
            pltpu.VMEM((total, width), BF16),
            pltpu.VMEM((total, width), BF16),
            pltpu.VMEM((steps, per, width), F32),
            pltpu.VMEM((steps, per, width), F32),
            *tiles_of(steps, tile, width),
            *tiles_of(steps, tile, width),
        ],
        steps,
        [pl.BlockSpec((total // 2, tile), lambda i: (0, i))] * 2,
    )


def weight_back(me, pieces, tokens, mask, tile, left, right, earlier=None):
    total, depth = tokens.shape
    block = depth // mask.shape[0]
    width = mask.shape[1] * block
    steps, slots = (right - left) // tile, 6
    known = [] if earlier is None else [earlier]

    def body(me_ref, x_ref, m_ref, *refs):
        refs, (out, mark, x_t, a_s, stage, sems) = refs[:-6], refs[-6:]
        mark[...] = jnp.zeros_like(mark)

        def leave(i):
            at = slice(left + i * tile, left + (i + 1) * tile)
            return pltpu.make_async_copy(stage.at[i % slots], out.at[:, at], sems.at[i % slots])

        x_t[...] = x_ref[...].T
        ways = (True, False) if left == 0 else (False,)
        join_halves(me_ref[0], [(way, *refs[2 * n : 2 * n + 2]) for n, way in enumerate(ways[: len(pieces) // 2])], a_s)
        m = spread(m_ref[...], block)[:, left:right]
        for i in range(steps):
            at = slice(i * tile, (i + 1) * tile)
            if i >= slots:
                leave(i - slots).wait()
            masked_product(x_t, a_s[:, at], m[:, at], stage.at[i % slots], block)
            leave(i).start()
        for i in range(max(steps - slots, 0), steps):
            leave(i).wait()

    return call(
        body,
        "weight_back",
        (me, tokens, mask, *pieces, *known),
        "svv" + "v" * len(pieces) + "h" * len(known),
        [shaped(depth, width, kind=BF16), shaped(8, 128)],
        "hv",
        [
            pltpu.VMEM((depth, total), BF16),
            pltpu.VMEM((total, right - left), BF16),
            *tiles_of(slots, depth, tile),
        ],
        aliases={3 + len(pieces): 0} if known else {},
    )


def swap(value, axis, size, bit):
    return lax.ppermute(value, axis, [(i, i ^ bit) for i in range(size)])


def after(value, *earlier):
    return lax.optimization_barrier((value, *earlier))[0]


def local(rows, cols, tokens_in, grad_out, gate_w, up_w, down_w, gate_mask, up_mask, down_mask):
    me = lax.axis_index("row").astype(jnp.int32)[None]
    width = gate_w.shape[1]
    tile = 256 if width % 256 == 0 else 128
    wide = 512 if width % 512 == 0 else 128

    def over_row(value, bit):
        return swap(value, "row", rows, bit)

    def over_col(value, bit):
        return swap(value, "col", cols, bit)

    def halve(total):
        half = total.shape[0] // 2
        return total[:half], total[half:].astype(BF16)

    def gathering(own):
        bit = cols // 2
        while bit:
            got = over_col(own, bit)
            earlier = yield own
            got = got if earlier is None else after(got, earlier)
            own = jnp.concatenate([own, got], axis=0)
            bit //= 2
        yield own

    def leaving(send, keep):
        bit = 1
        while bit < cols:
            got = over_col(send, bit)
            earlier = yield send
            keep = keep + (got if earlier is None else after(got, earlier))
            bit *= 2
            if bit < cols:
                keep, send = halve(keep)
        yield keep.astype(BF16)

    def last(rounds):
        for value in rounds:
            pass
        return value

    rounds = gathering(tokens_in)
    near = tokens = next(rounds)
    for value in rounds:
        near, tokens = tokens, value
    rounds = gathering(after(grad_out, near))
    next(rounds)
    gate_send, gate_keep = forward_part(me, tokens, gate_w, gate_mask, wide, True)
    gate_got = over_row(gate_send, 1)
    rounds.send(gate_send)
    up_send, up_keep = forward_part(after(me, gate_send), tokens, up_w, up_mask, wide, False)
    up_got = over_row(up_send, 2)
    rounds.send(up_send)
    grads = last(rounds)
    a_send, a_keep, b_send, b_keep = hidden_part(
        after(me, up_send), grads, down_w, after(down_mask, gate_send), wide
    )
    a_got, b_got = over_row(a_send, 1), over_row(b_send, 2)
    gate_got, up_got, a_send = lax.optimization_barrier((gate_got, up_got, a_send))
    gate_keep, gate_send = halve(gate_keep + gate_got)
    up_keep, up_send = halve(up_keep + up_got)
    gate_got, up_got = over_row(gate_send, 2), over_row(up_send, 1)

    def near_halves(front, rest, *earlier):
        front, rest = lax.optimization_barrier((front, rest, *earlier))[:2]
        return front, over_row(front, 2), rest, over_row(rest, 1)

    def all_halves(front, front_got, rest, rest_got, *earlier):
        front_got, rest_got = lax.optimization_barrier((front_got, rest_got, *earlier))[:2]
        front = jnp.concatenate([front, front_got], axis=0)
        rest = jnp.concatenate([rest, rest_got], axis=0)
        return front, over_row(front, 1), rest, over_row(rest, 2)

    front = a_keep.shape[1]
    gate_pre, up_pre = gate_keep + gate_got, up_keep + up_got
    hidden = (jax.nn.sigmoid(gate_pre) * gate_pre * up_pre).astype(BF16)
    hidden_a, hidden_b, gate_pre, up_pre = lax.optimization_barrier(
        (hidden[:, :front], hidden[:, front:], gate_pre, up_pre)
    )
    hidden_all = all_halves(*near_halves(hidden_a, hidden_b))

    a_keep, a_send = halve(a_keep + after(a_got, gate_send, up_send))
    b_keep, b_send = halve(b_keep + after(b_got, gate_send, up_send))
    a_got, b_got = over_row(a_send, 2), over_row(b_send, 1)
    a_got, b_got = after(a_got, hidden_a), after(b_got, hidden_a)
    pre = []
    for at, grad_hidden in ((slice(None, front), a_keep + a_got), (slice(front, None), b_keep + b_got)):
        gate, up = gate_pre[:, at], up_pre[:, at]
        sig = jax.nn.sigmoid(gate)
        pre.append((grad_hidden * up * sig * (1.0 + gate * (1.0 - sig))).astype(BF16))
        pre.append((grad_hidden * (gate * sig)).astype(BF16))
    gate_near = near_halves(pre[0], pre[2], hidden_all[0], hidden_all[2])
    gate_all = all_halves(*gate_near, hidden_all[1], hidden_all[3])
    up_near = near_halves(pre[1], pre[3], gate_all[0], gate_all[2])
    grad_down, out_send, out_keep = down_back(
        after(me, gate_all[0], gate_all[2]), hidden_all, grads, down_w, down_mask, 256
    )
    up_all = all_halves(*up_near, out_send)
    gate_all = lax.optimization_barrier((*gate_all, out_send, up_all[0], up_all[2]))[:4]
    out_rounds = leaving(out_send, out_keep)
    next(out_rounds)
    grad_gate, mark = weight_back(
        after(me, out_send), gate_all, tokens, gate_mask, tile, 0, width
    )
    out_send = out_rounds.send(mark)
    up_all = lax.optimization_barrier((*up_all, mark))[:4]
    in_send, in_keep = input_back(
        after(me, mark, out_send), gate_all, up_all, gate_w, up_w, gate_mask, up_mask, 256
    )
    out_send = out_rounds.send(in_send)
    in_rounds = leaving(in_send, in_keep)
    next(in_rounds)
    in_send = in_rounds.send(None)
    grad_up, mark = weight_back(
        after(me, in_send, out_send), up_all[:2], tokens, up_mask, tile, 0, front
    )
    layer_out = out_rounds.send(mark)
    in_send = in_rounds.send(mark)
    grad_up, mark = weight_back(
        after(me, in_send), up_all[2:], tokens, up_mask, tile, front, width, grad_up
    )
    if cols > 8:
        layer_out = last(out_rounds)
    grad_in = in_rounds.send(mark)
    if cols > 8:
        grad_in = last(in_rounds)
    return (layer_out, grad_in, grad_gate, grad_up, grad_down)


def solution(mesh):
    by_row, by_col = P("row", "col"), P("col", "row")
    return jax.shard_map(
        functools.partial(local, mesh.shape["row"], mesh.shape["col"]),
        mesh=mesh,
        in_specs=(by_col, by_col, by_row, by_row, by_col, by_row, by_row, by_col),
        out_specs=(by_col, by_col, by_row, by_row, by_col),
        check_vma=False,
    )
```

```python
import functools

import jax
import jax.numpy as jnp
from jax import lax
from jax.experimental import pallas as pl
from jax.experimental.pallas import tpu as pltpu
from jax.sharding import PartitionSpec as P

BF16 = jnp.bfloat16
F32 = jnp.float32
VMEM_LIMIT = 56 * 1024 * 1024
NT = (((1,), (1,)), ((), ()))


def dot(a, b):
    return jnp.dot(a, b, preferred_element_type=F32)


def spread(mask, block):
    count = mask.shape[1]
    shape = (count, count * block)
    col = lax.broadcasted_iota(jnp.int32, shape, 1) // block
    row = lax.broadcasted_iota(jnp.int32, shape, 0)
    return dot(mask.astype(BF16), jnp.where(row == col, 1.0, 0.0).astype(BF16))


def masked(w, m, block):
    return jnp.concatenate(
        [
            w[i * block : (i + 1) * block, :]
            * jnp.broadcast_to(m[i : i + 1, :], (block, w.shape[1])).astype(BF16)
            for i in range(w.shape[0] // block)
        ],
        axis=0,
    )


def masked_product(left, right, m, out, block):
    height = left.shape[0]
    some = 256 if height % 256 == 0 else 128
    for top in range(0, height, some):
        got = dot(left[top : top + some, :], right)
        for i in range(some // block):
            line = top // block + i
            out[top + i * block : top + (i + 1) * block, :] = (
                got[i * block : (i + 1) * block, :] * m[line : line + 1, :]
            ).astype(BF16)


def fetches(pairs, columns, size):
    def copy(pair, i):
        source, held, sems = pair
        at = slice(i * size, (i + 1) * size)
        return pltpu.make_async_copy(
            source.at[:, at] if columns else source.at[at, :], held.at[i], sems.at[i]
        )

    def begin():
        for i in range(pairs[0][1].shape[0]):
            for pair in pairs:
                copy(pair, i).start()

    def arrived(i):
        for pair in pairs:
            copy(pair, i).wait()

    return begin, arrived


def at_step(pairs, columns, size, prepare):
    begin, arrived = fetches(pairs, columns, size)
    step = pl.program_id(0)

    @pl.when(step == 0)
    def _():
        begin()
        prepare()

    for i in range(pairs[0][1].shape[0]):
        pl.when(step == i)(functools.partial(arrived, i))
    return step


def spread_steps(mask, block, columns, out):
    full = spread(mask, block)
    steps, height, width = out.shape
    for i in range(steps):
        if columns:
            out[i] = full[:, i * width : (i + 1) * width]
        else:
            out[i] = full[i * height : (i + 1) * height, :]


def order_by_row(me, source, out):
    quarter = out.shape[0] // 4
    for j in range(4):
        at = pl.ds(pl.multiple_of((me ^ j) * quarter, 16), quarter)
        out[j * quarter : (j + 1) * quarter, :] = source[at, :]


def join_halves(me, pieces, out):
    quarter = out.shape[0] // 4
    left = 0
    for x_first, near, far in pieces:
        at = slice(left, left + near.shape[1])
        left += near.shape[1]
        for half, spots in (
            (near, (0, 2) if x_first else (0, 1)),
            (far, (1, 3) if x_first else (2, 3)),
        ):
            for slot, j in enumerate(spots):
                rows = pl.ds(pl.multiple_of((me ^ j) * quarter, 16), quarter)
                out[rows, at] = half[slot * quarter : (slot + 1) * quarter, :]


def put_halves(part, send, keep, at, x_first):
    quarter = part.shape[0] // 4
    kept, sent = ((0, 2), (1, 3)) if x_first else ((0, 1), (2, 3))
    for slot in range(2):
        rows = slice(slot * quarter, (slot + 1) * quarter)
        keep[rows, at] = part[kept[slot] * quarter : (kept[slot] + 1) * quarter, :]
        send[rows, at] = part[sent[slot] * quarter : (sent[slot] + 1) * quarter, :].astype(BF16)


def call(body, name, inputs, kinds, outs, out_kinds, scratch, steps=None, maps=None, aliases={}, macs=500, marks=()):
    spec = {
        "s": pl.BlockSpec(memory_space=pltpu.SMEM),
        "v": pl.BlockSpec(memory_space=pltpu.VMEM),
        "h": pl.BlockSpec(memory_space=pl.ANY),
    }
    out_specs = [spec[kind] for kind in out_kinds] if maps is None else maps
    grid = {} if steps is None else {"grid": (steps,)}

    def unmarked(*refs):
        body(*refs[: len(inputs)], *refs[len(inputs) + len(marks) :])

    return pl.pallas_call(
        unmarked,
        in_specs=[spec[kind] for kind in (*kinds, *"h" * len(marks))],
        out_specs=out_specs,
        out_shape=outs,
        scratch_shapes=scratch,
        input_output_aliases=aliases,
        compiler_params=pltpu.CompilerParams(vmem_limit_bytes=VMEM_LIMIT),
        cost_estimate=pl.CostEstimate(flops=2 * macs, bytes_accessed=1000, transcendentals=0),
        name=name,
        **grid,
    )(*inputs, *marks)


def tiles_of(count, height, width):
    return [pltpu.VMEM((count, height, width), BF16), pltpu.SemaphoreType.DMA((count,))]


def shaped(*shape, kind=F32):
    return jax.ShapeDtypeStruct(shape, kind)


def parts_of(tile):
    some = min(tile, 256)
    return [slice(left, left + some) for left in range(0, tile, some)]


def forward_part(me, tokens, weight, mask, tile, x_first):
    total, depth = tokens.shape
    width = weight.shape[1]
    steps = width // tile
    block = depth // mask.shape[0]

    def body(me_ref, x_ref, w_hbm, m_ref, send, keep, x_s, m_s, held, sems):
        def prepare():
            order_by_row(me_ref[0], x_ref, x_s)
            spread_steps(m_ref[...], block, True, m_s)

        step = at_step([(w_hbm, held, sems)], True, tile, prepare)
        w, m = held.at[step], m_s[step]
        for at in parts_of(tile):
            part = dot(x_s[...], masked(w.at[:, at], m[:, at], block))
            put_halves(part, send, keep, at, x_first)

    return call(
        body,
        "forward_part",
        (me, tokens, weight, mask),
        "svhv",
        [shaped(total // 2, width, kind=BF16), shaped(total // 2, width)],
        None,
        [
            pltpu.VMEM((total, depth), BF16),
            pltpu.VMEM((steps, mask.shape[0], tile), F32),
            *tiles_of(steps, depth, tile),
        ],
        steps,
        [pl.BlockSpec((total // 2, tile), lambda i: (0, i))] * 2,
    )


def hidden_part(me, grads, weight, mask, tile):
    total, depth = grads.shape
    steps = weight.shape[0] // tile
    front = (steps + 1) // 2
    block = depth // mask.shape[1]
    per = tile // block

    def body(me_ref, x_ref, w_hbm, m_ref, a_send, a_keep, b_send, b_keep, x_s, m_s, held, sems):
        def prepare():
            order_by_row(me_ref[0], x_ref, x_s)
            spread_steps(m_ref[...], block, False, m_s)

        step = at_step([(w_hbm, held, sems)], False, tile, prepare)
        w, m = held.at[step], m_s[step]

        def put(send, keep, x_first):
            for at in parts_of(tile):
                rows = slice(at.start // block, at.stop // block)
                part = lax.dot_general(
                    x_s[...], masked(w.at[at, :], m[rows, :], block), NT, preferred_element_type=F32
                )
                put_halves(part, send, keep, at, x_first)

        pl.when(step < front)(functools.partial(put, a_send, a_keep, True))
        pl.when(step >= front)(functools.partial(put, b_send, b_keep, False))

    return call(
        body,
        "hidden_part",
        (me, grads, weight, mask),
        "svhv",
        [
            shaped(total // 2, count * tile, kind=kind)
            for count in (front, steps - front)
            for kind in (BF16, F32)
        ],
        None,
        [
            pltpu.VMEM((total, depth), BF16),
            pltpu.VMEM((steps, per, depth), F32),
            *tiles_of(steps, tile, depth),
        ],
        steps,
        [pl.BlockSpec((total // 2, tile), lambda i: (0, jnp.minimum(i, front - 1)))] * 2
        + [pl.BlockSpec((total // 2, tile), lambda i: (0, jnp.maximum(i - front, 0)))] * 2,
    )


def down_back(me, pieces, grads, weight, mask, tile):
    total, depth = grads.shape
    width = weight.shape[0]
    block = width // mask.shape[0]
    steps, slots = depth // tile, 4

    def body(me_ref, h0, h1, h2, h3, g_ref, w_hbm, m_ref, gw, send, keep, hid, hid_t, held, sems, stage, outs):
        begin, arrived = fetches([(w_hbm, held, sems)], True, tile)
        begin()
        join_halves(me_ref[0], ((True, h0, h1), (False, h2, h3)), hid)
        hid_t[...] = hid[...].T
        m = spread(m_ref[...], block)

        def leave(i):
            at = slice(i * tile, (i + 1) * tile)
            return pltpu.make_async_copy(stage.at[i % slots], gw.at[:, at], outs.at[i % slots])

        arrived(0)
        w = masked(held.at[0], m[:, :tile], block)
        for i in range(steps):
            at = slice(i * tile, (i + 1) * tile)
            now = w
            if i >= slots:
                leave(i - slots).wait()
            if i + 1 < steps:
                arrived(i + 1)
                w = masked(held.at[i + 1], m[:, (i + 1) * tile : (i + 2) * tile], block)
            out = dot(hid[...], now)
            keep[:, at] = out[: total // 2, :]
            send[:, at] = out[total // 2 :, :]
            masked_product(hid_t, g_ref[:, at], m[:, at], stage.at[i % slots], block)
            leave(i).start()
        for i in range(max(steps - slots, 0), steps):
            leave(i).wait()

    return call(
        body,
        "down_back",
        (me, *pieces, grads, weight, mask),
        "svvvvvhv",
        [shaped(width, depth, kind=BF16), shaped(total // 2, depth), shaped(total // 2, depth)],
        "hvv",
        [
            pltpu.VMEM((total, width), BF16),
            pltpu.VMEM((width, total), BF16),
            *tiles_of(steps, width, tile),
            pltpu.VMEM((slots, width, tile), BF16),
            pltpu.SemaphoreType.DMA((slots,)),
        ],
        macs=2 * total * depth * width,
    )


def input_back(me, gate_pieces, up_pieces, gate_w, up_w, gate_m, up_m, tile, marks=()):
    depth, width = gate_w.shape
    total = 2 * gate_pieces[0].shape[0]
    block = depth // gate_m.shape[0]
    steps, per = depth // tile, tile // block

    def body(me_ref, *refs):
        pieces, (gw, uw, gm, um, send, keep, a_s, b_s, gm_s, um_s, gh, gs, uh, us) = refs[:8], refs[8:]

        def prepare():
            join_halves(me_ref[0], ((True, *pieces[0:2]), (False, *pieces[2:4])), a_s)
            join_halves(me_ref[0], ((True, *pieces[4:6]), (False, *pieces[6:8])), b_s)
            spread_steps(gm[...], block, False, gm_s)
            spread_steps(um[...], block, False, um_s)

        step = at_step([(gw, gh, gs), (uw, uh, us)], False, tile, prepare)
        out = lax.dot_general(
            a_s[...], masked(gh.at[step], gm_s[step], block), NT, preferred_element_type=F32
        )
        out += lax.dot_general(
            b_s[...], masked(uh.at[step], um_s[step], block), NT, preferred_element_type=F32
        )
        keep[...] = out[: total // 2, :]
        send[...] = out[total // 2 :, :]

    return call(
        body,
        "input_back",
        (me, *gate_pieces, *up_pieces, gate_w, up_w, gate_m, up_m),
        "s" + "v" * 8 + "hhvv",
        [shaped(total // 2, depth), shaped(total // 2, depth)],
        None,
        [
            pltpu.VMEM((total, width), BF16),
            pltpu.VMEM((total, width), BF16),
            pltpu.VMEM((steps, per, width), F32),
            pltpu.VMEM((steps, per, width), F32),
            *tiles_of(steps, tile, width),
            *tiles_of(steps, tile, width),
        ],
        steps,
        [pl.BlockSpec((total // 2, tile), lambda i: (0, i))] * 2,
        macs=2 * total * depth * width,
        marks=marks,
    )


def weight_back(me, pieces, tokens, mask, tile, left, right, earlier=None, marks=()):
    total, depth = tokens.shape
    block = depth // mask.shape[0]
    width = mask.shape[1] * block
    steps, slots = depth // tile, 6
    known = [] if earlier is None else [earlier]

    def body(me_ref, x_ref, m_ref, *refs):
        refs, (out, mark, a_s, stage, sems) = refs[:-5], refs[-5:]
        mark[...] = jnp.zeros_like(mark)

        def leave(i):
            rows = slice(i * tile, (i + 1) * tile)
            return pltpu.make_async_copy(
                stage.at[i % slots], out.at[rows, left:right], sems.at[i % slots]
            )

        ways = (True, False) if left == 0 else (False,)
        join_halves(
            me_ref[0],
            [(way, *refs[2 * n : 2 * n + 2]) for n, way in enumerate(ways[: len(pieces) // 2])],
            a_s,
        )
        m = spread(m_ref[...], block)[:, left:right]
        for i in range(steps):
            if i >= slots:
                leave(i - slots).wait()
            got = lax.dot_general(
                x_ref[:, i * tile : (i + 1) * tile],
                a_s[...],
                (((0,), (0,)), ((), ())),
                preferred_element_type=F32,
            )
            for j in range(tile // block):
                line = i * (tile // block) + j
                stage[i % slots, j * block : (j + 1) * block, :] = (
                    got[j * block : (j + 1) * block, :] * m[line : line + 1, :]
                ).astype(BF16)
            leave(i).start()
        for i in range(max(steps - slots, 0), steps):
            leave(i).wait()

    return call(
        body,
        "weight_back",
        (me, tokens, mask, *pieces, *known),
        "svv" + "v" * len(pieces) + "h" * len(known),
        [shaped(depth, width, kind=BF16), shaped(8, 128)],
        "hv",
        [pltpu.VMEM((total, right - left), BF16), *tiles_of(slots, tile, right - left)],
        aliases={3 + len(pieces): 0} if known else {},
        macs=total * depth * (right - left),
        marks=marks,
    )


def swap(value, axis, size, bit):
    return lax.ppermute(value, axis, [(i, i ^ bit) for i in range(size)])


def after(value, *earlier):
    return lax.optimization_barrier((value, *earlier))[0]


def local(rows, cols, tokens_in, grad_out, gate_w, up_w, down_w, gate_mask, up_mask, down_mask):
    me = lax.axis_index("row").astype(jnp.int32)[None]
    width = gate_w.shape[1]
    wide = 512 if width % 512 == 0 else 128

    def over_row(value, bit):
        return swap(value, "row", rows, bit)

    def over_col(value, bit):
        return swap(value, "col", cols, bit)

    def halve(total):
        half = total.shape[0] // 2
        return total[:half], total[half:].astype(BF16)

    def gathering(own):
        bit = cols // 2
        while bit:
            got = over_col(own, bit)
            earlier = yield own
            got = got if earlier is None else after(got, earlier)
            own = jnp.concatenate([own, got], axis=0)
            bit //= 2
        yield own

    def leaving(send, keep):
        bit, earlier = 1, None
        while bit < cols:
            got = over_col(send, bit)
            earlier = yield send, earlier
            if earlier is not None:
                got, earlier = lax.optimization_barrier((got, earlier))
            keep = keep + got
            bit *= 2
            if bit < cols:
                keep, send = halve(keep)
        yield keep.astype(BF16), earlier

    def last(rounds):
        for value in rounds:
            pass
        return value

    rounds = gathering(tokens_in)
    near = tokens = next(rounds)
    for value in rounds:
        near, tokens = tokens, value
    rounds = gathering(after(grad_out, near))
    next(rounds)
    gate_send, gate_keep = forward_part(me, tokens, gate_w, gate_mask, wide, True)
    gate_got = over_row(gate_send, 1)
    rounds.send(gate_send)
    up_send, up_keep = forward_part(after(me, gate_send), tokens, up_w, up_mask, wide, False)
    up_got = over_row(up_send, 2)
    rounds.send(up_send)
    grads = last(rounds)
    a_send, a_keep, b_send, b_keep = hidden_part(
        after(me, up_send), grads, down_w, after(down_mask, gate_send), wide
    )
    a_got, b_got = over_row(a_send, 1), over_row(b_send, 2)
    gate_got, up_got, a_send = lax.optimization_barrier((gate_got, up_got, a_send))
    gate_keep, gate_send = halve(gate_keep + gate_got)
    up_keep, up_send = halve(up_keep + up_got)
    gate_got, up_got = over_row(gate_send, 2), over_row(up_send, 1)

    def near_halves(front, rest, *earlier):
        front, rest = lax.optimization_barrier((front, rest, *earlier))[:2]
        return front, over_row(front, 2), rest, over_row(rest, 1)

    def all_halves(front, front_got, rest, rest_got, *earlier):
        front_got, rest_got = lax.optimization_barrier((front_got, rest_got, *earlier))[:2]
        front = jnp.concatenate([front, front_got], axis=0)
        rest = jnp.concatenate([rest, rest_got], axis=0)
        return front, over_row(front, 1), rest, over_row(rest, 2)

    front = a_keep.shape[1]
    gate_pre, up_pre = gate_keep + gate_got, up_keep + up_got
    hidden = (jax.nn.sigmoid(gate_pre) * gate_pre * up_pre).astype(BF16)
    hidden_a, hidden_b, gate_pre, up_pre = lax.optimization_barrier(
        (hidden[:, :front], hidden[:, front:], gate_pre, up_pre)
    )
    hidden_all = all_halves(*near_halves(hidden_a, hidden_b))

    a_keep, a_send = halve(a_keep + after(a_got, gate_send, up_send))
    b_keep, b_send = halve(b_keep + after(b_got, gate_send, up_send))
    a_got, b_got = over_row(a_send, 2), over_row(b_send, 1)
    a_got, b_got = after(a_got, hidden_a), after(b_got, hidden_a)
    pre = []
    for at, grad_hidden in ((slice(None, front), a_keep + a_got), (slice(front, None), b_keep + b_got)):
        gate, up = gate_pre[:, at], up_pre[:, at]
        sig = jax.nn.sigmoid(gate)
        pre.append((grad_hidden * up * sig * (1.0 + gate * (1.0 - sig))).astype(BF16))
        pre.append((grad_hidden * (gate * sig)).astype(BF16))
    gate_near = near_halves(pre[0], pre[2], hidden_all[0], hidden_all[2])
    gate_all = all_halves(*gate_near, hidden_all[1], hidden_all[3])
    up_near = near_halves(pre[1], pre[3], gate_all[0], gate_all[2])
    grad_down, out_send, out_keep = down_back(
        after(me, gate_all[0], gate_all[2]), hidden_all, grads, down_w, down_mask, 256
    )
    up_near = list(up_near)
    up_near[1], up_near[3], out_send = lax.optimization_barrier((up_near[1], up_near[3], out_send))
    up_all = all_halves(*up_near)
    out_rounds = leaving(out_send, out_keep)
    next(out_rounds)
    grad_gate, mark = weight_back(
        after(me, out_send), gate_all[:2], tokens, gate_mask, 256, 0, front
    )
    _, mark = out_rounds.send(mark)
    grad_gate, mark = weight_back(
        me, gate_all[2:], tokens, gate_mask, 256, front, width, grad_gate, [mark]
    )
    _, mark = out_rounds.send(mark)
    in_send, in_keep = input_back(
        me, gate_all, up_all, gate_w, up_w, gate_mask, up_mask, 256, [mark]
    )
    layer_out, in_send = out_rounds.send(in_send)
    in_rounds = leaving(in_send, in_keep)
    next(in_rounds)
    in_send, _ = in_rounds.send(None)
    grad_up, mark = weight_back(
        after(me, in_send), up_all[:2], tokens, up_mask, 256, 0, front
    )
    in_send, mark = in_rounds.send(mark)
    grad_up, mark = weight_back(
        after(me, in_send), up_all[2:], tokens, up_mask, 256, front, width, grad_up, [mark]
    )
    grad_in, _ = in_rounds.send(None)
    if cols > 8:
        (layer_out, _), (grad_in, _) = last(out_rounds), last(in_rounds)
    return (layer_out, grad_in, grad_gate, grad_up, grad_down)


def solution(mesh):
    by_row, by_col = P("row", "col"), P("col", "row")
    return jax.shard_map(
        functools.partial(local, mesh.shape["row"], mesh.shape["col"]),
        mesh=mesh,
        in_specs=(by_col, by_col, by_row, by_row, by_col, by_row, by_row, by_col),
        out_specs=(by_col, by_col, by_row, by_row, by_col),
        check_vma=False,
    )
```

```python
import functools

import jax
import jax.numpy as jnp
from jax import lax
from jax.experimental import pallas as pl
from jax.experimental.pallas import tpu as pltpu
from jax.sharding import PartitionSpec as P

BF16 = jnp.bfloat16
F32 = jnp.float32
VMEM_LIMIT = 56 * 1024 * 1024
AHEAD = 3
NT = (((1,), (1,)), ((), ()))


def dot(a, b):
    return jnp.dot(a, b, preferred_element_type=F32)


def spread(mask, block):
    count = mask.shape[1]
    shape = (count, count * block)
    col = lax.broadcasted_iota(jnp.int32, shape, 1) // block
    row = lax.broadcasted_iota(jnp.int32, shape, 0)
    return dot(mask.astype(BF16), jnp.where(row == col, 1.0, 0.0).astype(BF16))


def masked(w, m, block):
    return jnp.concatenate(
        [
            w[i * block : (i + 1) * block, :]
            * jnp.broadcast_to(m[i : i + 1, :], (block, w.shape[1])).astype(BF16)
            for i in range(w.shape[0] // block)
        ],
        axis=0,
    )


def masked_product(left, right, m, out, block):
    height = left.shape[0]
    some = 256 if height % 256 == 0 else 128
    for top in range(0, height, some):
        got = dot(left[top : top + some, :], right)
        for i in range(some // block):
            line = top // block + i
            out[top + i * block : top + (i + 1) * block, :] = (
                got[i * block : (i + 1) * block, :] * m[line : line + 1, :]
            ).astype(BF16)


def fetches(pairs, columns, size):
    def copy(pair, i):
        source, held, sems = pair
        at = slice(i * size, (i + 1) * size)
        return pltpu.make_async_copy(
            source.at[:, at] if columns else source.at[at, :], held.at[i], sems.at[i]
        )

    def begin(i):
        for pair in pairs:
            copy(pair, i).start()

    def arrived(i):
        for pair in pairs:
            copy(pair, i).wait()

    return begin, arrived


def at_step(pairs, columns, size, prepare):
    begin, arrived = fetches(pairs, columns, size)
    step, steps = pl.program_id(0), pairs[0][1].shape[0]

    @pl.when(step == 0)
    def _():
        for i in range(min(AHEAD, steps)):
            begin(i)
        prepare()

    for i in range(steps):

        @pl.when(step == i)
        def _(i=i):
            if i + AHEAD < steps:
                begin(i + AHEAD)
            arrived(i)

    return step


def spread_steps(mask, block, columns, out):
    full = spread(mask, block)
    steps, height, width = out.shape
    for i in range(steps):
        if columns:
            out[i] = full[:, i * width : (i + 1) * width]
        else:
            out[i] = full[i * height : (i + 1) * height, :]


def order_by_row(me, source, out):
    quarter = out.shape[0] // 4
    for j in range(4):
        at = pl.ds(pl.multiple_of((me ^ j) * quarter, 16), quarter)
        out[j * quarter : (j + 1) * quarter, :] = source[at, :]


def join_halves(me, pieces, out):
    quarter = out.shape[0] // 4
    left = 0
    for x_first, near, far in pieces:
        at = slice(left, left + near.shape[1])
        left += near.shape[1]
        for half, spots in (
            (near, (0, 2) if x_first else (0, 1)),
            (far, (1, 3) if x_first else (2, 3)),
        ):
            for slot, j in enumerate(spots):
                rows = pl.ds(pl.multiple_of((me ^ j) * quarter, 16), quarter)
                out[rows, at] = half[slot * quarter : (slot + 1) * quarter, :]


def put_halves(part, send, keep, at, x_first):
    quarter = part.shape[0] // 4
    kept, sent = ((0, 2), (1, 3)) if x_first else ((0, 1), (2, 3))
    for slot in range(2):
        rows = slice(slot * quarter, (slot + 1) * quarter)
        keep[rows, at] = part[kept[slot] * quarter : (kept[slot] + 1) * quarter, :]
        send[rows, at] = part[sent[slot] * quarter : (sent[slot] + 1) * quarter, :].astype(BF16)


def call(body, name, inputs, kinds, outs, out_kinds, scratch, steps=None, maps=None, aliases={}, macs=500, marks=()):
    spec = {
        "s": pl.BlockSpec(memory_space=pltpu.SMEM),
        "v": pl.BlockSpec(memory_space=pltpu.VMEM),
        "h": pl.BlockSpec(memory_space=pl.ANY),
    }
    out_specs = [spec[kind] for kind in out_kinds] if maps is None else maps
    grid = {} if steps is None else {"grid": (steps,)}

    def unmarked(*refs):
        body(*refs[: len(inputs)], *refs[len(inputs) + len(marks) :])

    return pl.pallas_call(
        unmarked,
        in_specs=[spec[kind] for kind in (*kinds, *"h" * len(marks))],
        out_specs=out_specs,
        out_shape=outs,
        scratch_shapes=scratch,
        input_output_aliases=aliases,
        compiler_params=pltpu.CompilerParams(vmem_limit_bytes=VMEM_LIMIT),
        cost_estimate=pl.CostEstimate(flops=2 * macs, bytes_accessed=1000, transcendentals=0),
        name=name,
        **grid,
    )(*inputs, *marks)


def tiles_of(count, height, width):
    return [pltpu.VMEM((count, height, width), BF16), pltpu.SemaphoreType.DMA((count,))]


def shaped(*shape, kind=F32):
    return jax.ShapeDtypeStruct(shape, kind)


def parts_of(tile):
    some = min(tile, 256)
    return [slice(left, left + some) for left in range(0, tile, some)]


def forward_part(me, tokens, weight, mask, tile, x_first):
    total, depth = tokens.shape
    width = weight.shape[1]
    steps = width // tile
    block = depth // mask.shape[0]

    def body(me_ref, x_ref, w_hbm, m_ref, send, keep, x_s, m_s, held, sems):
        def prepare():
            order_by_row(me_ref[0], x_ref, x_s)
            spread_steps(m_ref[...], block, True, m_s)

        step = at_step([(w_hbm, held, sems)], True, tile, prepare)
        w, m = held.at[step], m_s[step]
        for at in parts_of(tile):
            part = dot(x_s[...], masked(w.at[:, at], m[:, at], block))
            put_halves(part, send, keep, at, x_first)

    return call(
        body,
        "forward_part",
        (me, tokens, weight, mask),
        "svhv",
        [shaped(total // 2, width, kind=BF16), shaped(total // 2, width)],
        None,
        [
            pltpu.VMEM((total, depth), BF16),
            pltpu.VMEM((steps, mask.shape[0], tile), F32),
            *tiles_of(steps, depth, tile),
        ],
        steps,
        [pl.BlockSpec((total // 2, tile), lambda i: (0, i))] * 2,
    )


def hidden_part(me, grads, weight, mask, tile):
    total, depth = grads.shape
    steps = weight.shape[0] // tile
    front = (steps + 1) // 2
    block = depth // mask.shape[1]
    per = tile // block

    def body(me_ref, x_ref, w_hbm, m_ref, a_send, a_keep, b_send, b_keep, x_s, m_s, held, sems):
        def prepare():
            order_by_row(me_ref[0], x_ref, x_s)
            spread_steps(m_ref[...], block, False, m_s)

        step = at_step([(w_hbm, held, sems)], False, tile, prepare)
        w, m = held.at[step], m_s[step]

        def put(send, keep, x_first):
            for at in parts_of(tile):
                rows = slice(at.start // block, at.stop // block)
                part = lax.dot_general(
                    x_s[...], masked(w.at[at, :], m[rows, :], block), NT, preferred_element_type=F32
                )
                put_halves(part, send, keep, at, x_first)

        pl.when(step < front)(functools.partial(put, a_send, a_keep, True))
        pl.when(step >= front)(functools.partial(put, b_send, b_keep, False))

    return call(
        body,
        "hidden_part",
        (me, grads, weight, mask),
        "svhv",
        [
            shaped(total // 2, count * tile, kind=kind)
            for count in (front, steps - front)
            for kind in (BF16, F32)
        ],
        None,
        [
            pltpu.VMEM((total, depth), BF16),
            pltpu.VMEM((steps, per, depth), F32),
            *tiles_of(steps, tile, depth),
        ],
        steps,
        [pl.BlockSpec((total // 2, tile), lambda i: (0, jnp.minimum(i, front - 1)))] * 2
        + [pl.BlockSpec((total // 2, tile), lambda i: (0, jnp.maximum(i - front, 0)))] * 2,
    )


def down_back(me, pieces, grads, weight, mask, tile):
    total, depth = grads.shape
    width = weight.shape[0]
    block = width // mask.shape[0]
    steps, slots = depth // tile, 4

    def body(me_ref, h0, h1, h2, h3, g_ref, w_hbm, m_ref, gw, send, keep, hid, hid_t, held, sems, stage, outs):
        begin, arrived = fetches([(w_hbm, held, sems)], True, tile)
        for i in range(min(AHEAD, steps)):
            begin(i)
        join_halves(me_ref[0], ((True, h0, h1), (False, h2, h3)), hid)
        hid_t[...] = hid[...].T
        m = spread(m_ref[...], block)

        def leave(i):
            at = slice(i * tile, (i + 1) * tile)
            return pltpu.make_async_copy(stage.at[i % slots], gw.at[:, at], outs.at[i % slots])

        arrived(0)
        w = masked(held.at[0], m[:, :tile], block)
        for i in range(steps):
            at = slice(i * tile, (i + 1) * tile)
            now = w
            if i >= slots:
                leave(i - slots).wait()
            if i + AHEAD < steps:
                begin(i + AHEAD)
            if i + 1 < steps:
                arrived(i + 1)
                w = masked(held.at[i + 1], m[:, (i + 1) * tile : (i + 2) * tile], block)
            out = dot(hid[...], now)
            keep[:, at] = out[: total // 2, :]
            send[:, at] = out[total // 2 :, :]
            masked_product(hid_t, g_ref[:, at], m[:, at], stage.at[i % slots], block)
            leave(i).start()
        for i in range(max(steps - slots, 0), steps):
            leave(i).wait()

    return call(
        body,
        "down_back",
        (me, *pieces, grads, weight, mask),
        "svvvvvhv",
        [shaped(width, depth, kind=BF16), shaped(total // 2, depth), shaped(total // 2, depth)],
        "hvv",
        [
            pltpu.VMEM((total, width), BF16),
            pltpu.VMEM((width, total), BF16),
            *tiles_of(steps, width, tile),
            pltpu.VMEM((slots, width, tile), BF16),
            pltpu.SemaphoreType.DMA((slots,)),
        ],
        macs=2 * total * depth * width,
    )


def input_back(me, gate_pieces, up_pieces, gate_w, up_w, gate_m, up_m, tile, marks=()):
    depth, width = gate_w.shape
    total = 2 * gate_pieces[0].shape[0]
    block = depth // gate_m.shape[0]
    steps, per = depth // tile, tile // block

    def body(me_ref, *refs):
        pieces, (gw, uw, gm, um, send, keep, a_s, b_s, gm_s, um_s, gh, gs, uh, us) = refs[:8], refs[8:]

        def prepare():
            join_halves(me_ref[0], ((True, *pieces[0:2]), (False, *pieces[2:4])), a_s)
            join_halves(me_ref[0], ((True, *pieces[4:6]), (False, *pieces[6:8])), b_s)
            spread_steps(gm[...], block, False, gm_s)
            spread_steps(um[...], block, False, um_s)

        step = at_step([(gw, gh, gs), (uw, uh, us)], False, tile, prepare)
        out = lax.dot_general(
            a_s[...], masked(gh.at[step], gm_s[step], block), NT, preferred_element_type=F32
        )
        out += lax.dot_general(
            b_s[...], masked(uh.at[step], um_s[step], block), NT, preferred_element_type=F32
        )
        keep[...] = out[: total // 2, :]
        send[...] = out[total // 2 :, :]

    return call(
        body,
        "input_back",
        (me, *gate_pieces, *up_pieces, gate_w, up_w, gate_m, up_m),
        "s" + "v" * 8 + "hhvv",
        [shaped(total // 2, depth), shaped(total // 2, depth)],
        None,
        [
            pltpu.VMEM((total, width), BF16),
            pltpu.VMEM((total, width), BF16),
            pltpu.VMEM((steps, per, width), F32),
            pltpu.VMEM((steps, per, width), F32),
            *tiles_of(steps, tile, width),
            *tiles_of(steps, tile, width),
        ],
        steps,
        [pl.BlockSpec((total // 2, tile), lambda i: (0, i))] * 2,
        macs=2 * total * depth * width,
        marks=marks,
    )


def weight_back(me, pieces, tokens, mask, tile, left, right, earlier=None, marks=()):
    total, depth = tokens.shape
    block = depth // mask.shape[0]
    width = mask.shape[1] * block
    steps, slots = depth // tile, 6
    known = [] if earlier is None else [earlier]

    def body(me_ref, x_ref, m_ref, *refs):
        refs, (out, mark, a_s, stage, sems) = refs[:-5], refs[-5:]
        mark[...] = jnp.zeros_like(mark)

        def leave(i):
            rows = slice(i * tile, (i + 1) * tile)
            return pltpu.make_async_copy(
                stage.at[i % slots], out.at[rows, left:right], sems.at[i % slots]
            )

        ways = (True, False) if left == 0 else (False,)
        join_halves(
            me_ref[0],
            [(way, *refs[2 * n : 2 * n + 2]) for n, way in enumerate(ways[: len(pieces) // 2])],
            a_s,
        )
        m = spread(m_ref[...], block)[:, left:right]
        for i in range(steps):
            if i >= slots:
                leave(i - slots).wait()
            got = lax.dot_general(
                x_ref[:, i * tile : (i + 1) * tile],
                a_s[...],
                (((0,), (0,)), ((), ())),
                preferred_element_type=F32,
            )
            for j in range(tile // block):
                line = i * (tile // block) + j
                stage[i % slots, j * block : (j + 1) * block, :] = (
                    got[j * block : (j + 1) * block, :] * m[line : line + 1, :]
                ).astype(BF16)
            leave(i).start()
        for i in range(max(steps - slots, 0), steps):
            leave(i).wait()

    return call(
        body,
        "weight_back",
        (me, tokens, mask, *pieces, *known),
        "svv" + "v" * len(pieces) + "h" * len(known),
        [shaped(depth, width, kind=BF16), shaped(8, 128)],
        "hv",
        [pltpu.VMEM((total, right - left), BF16), *tiles_of(slots, tile, right - left)],
        aliases={3 + len(pieces): 0} if known else {},
        macs=total * depth * (right - left),
        marks=marks,
    )


def swap(value, axis, size, bit):
    return lax.ppermute(value, axis, [(i, i ^ bit) for i in range(size)])


def after(value, *earlier):
    return lax.optimization_barrier((value, *earlier))[0]


def local(rows, cols, tokens_in, grad_out, gate_w, up_w, down_w, gate_mask, up_mask, down_mask):
    me = lax.axis_index("row").astype(jnp.int32)[None]
    width = gate_w.shape[1]
    wide = 512 if width % 512 == 0 else 128

    def over_row(value, bit):
        return swap(value, "row", rows, bit)

    def over_col(value, bit):
        return swap(value, "col", cols, bit)

    def halve(total):
        half = total.shape[0] // 2
        return total[:half], total[half:].astype(BF16)

    def gathering(own):
        bit = cols // 2
        while bit:
            got = over_col(own, bit)
            earlier = yield own
            got = got if earlier is None else after(got, earlier)
            own = jnp.concatenate([own, got], axis=0)
            bit //= 2
        yield own

    def leaving(send, keep):
        bit, earlier = 1, None
        while bit < cols:
            got = over_col(send, bit)
            earlier = yield send, earlier
            if earlier is not None:
                got, earlier = lax.optimization_barrier((got, earlier))
            keep = keep + got
            bit *= 2
            if bit < cols:
                keep, send = halve(keep)
        yield keep.astype(BF16), earlier

    def last(rounds):
        for value in rounds:
            pass
        return value

    rounds = gathering(tokens_in)
    near = tokens = next(rounds)
    for value in rounds:
        near, tokens = tokens, value
    rounds = gathering(after(grad_out, near))
    next(rounds)
    gate_send, gate_keep = forward_part(me, tokens, gate_w, gate_mask, wide, True)
    gate_got = over_row(gate_send, 1)
    rounds.send(gate_send)
    up_send, up_keep = forward_part(after(me, gate_send), tokens, up_w, up_mask, wide, False)
    up_got = over_row(up_send, 2)
    rounds.send(up_send)
    grads = last(rounds)
    a_send, a_keep, b_send, b_keep = hidden_part(
        after(me, up_send), grads, down_w, after(down_mask, gate_send), wide
    )
    a_got, b_got = over_row(a_send, 1), over_row(b_send, 2)
    gate_got, up_got, a_send = lax.optimization_barrier((gate_got, up_got, a_send))
    gate_keep, gate_send = halve(gate_keep + gate_got)
    up_keep, up_send = halve(up_keep + up_got)
    gate_got, up_got = over_row(gate_send, 2), over_row(up_send, 1)

    def near_halves(front, rest, *earlier):
        front, rest = lax.optimization_barrier((front, rest, *earlier))[:2]
        return front, over_row(front, 2), rest, over_row(rest, 1)

    def all_halves(front, front_got, rest, rest_got, *earlier):
        front_got, rest_got = lax.optimization_barrier((front_got, rest_got, *earlier))[:2]
        front = jnp.concatenate([front, front_got], axis=0)
        rest = jnp.concatenate([rest, rest_got], axis=0)
        return front, over_row(front, 1), rest, over_row(rest, 2)

    front = a_keep.shape[1]
    gate_pre, up_pre = gate_keep + gate_got, up_keep + up_got
    hidden = (jax.nn.sigmoid(gate_pre) * gate_pre * up_pre).astype(BF16)
    hidden_a, hidden_b, gate_pre, up_pre = lax.optimization_barrier(
        (hidden[:, :front], hidden[:, front:], gate_pre, up_pre)
    )
    hidden_all = all_halves(*near_halves(hidden_a, hidden_b))

    a_keep, a_send = halve(a_keep + after(a_got, gate_send, up_send))
    b_keep, b_send = halve(b_keep + after(b_got, gate_send, up_send))
    a_got, b_got = over_row(a_send, 2), over_row(b_send, 1)
    a_got, b_got = after(a_got, hidden_a), after(b_got, hidden_a)
    pre = []
    for at, grad_hidden in ((slice(None, front), a_keep + a_got), (slice(front, None), b_keep + b_got)):
        gate, up = gate_pre[:, at], up_pre[:, at]
        sig = jax.nn.sigmoid(gate)
        pre.append((grad_hidden * up * sig * (1.0 + gate * (1.0 - sig))).astype(BF16))
        pre.append((grad_hidden * (gate * sig)).astype(BF16))
    gate_near = near_halves(pre[0], pre[2], hidden_all[0], hidden_all[2])
    gate_all = all_halves(*gate_near, hidden_all[1], hidden_all[3])
    up_near = near_halves(pre[1], pre[3], gate_all[0], gate_all[2])
    grad_down, out_send, out_keep = down_back(
        after(me, gate_all[0], gate_all[2]), hidden_all, grads, down_w, down_mask, 256
    )
    up_near = list(up_near)
    up_near[1], up_near[3], out_send = lax.optimization_barrier((up_near[1], up_near[3], out_send))
    up_all = all_halves(*up_near)
    out_rounds = leaving(out_send, out_keep)
    next(out_rounds)
    grad_gate, mark = weight_back(
        after(me, out_send), gate_all[:2], tokens, gate_mask, 256, 0, front
    )
    _, mark = out_rounds.send(mark)
    grad_gate, mark = weight_back(
        me, gate_all[2:], tokens, gate_mask, 256, front, width, grad_gate, [mark]
    )
    _, mark = out_rounds.send(mark)
    in_send, in_keep = input_back(
        me, gate_all, up_all, gate_w, up_w, gate_mask, up_mask, 256, [mark]
    )
    layer_out, in_send = out_rounds.send(in_send)
    in_rounds = leaving(in_send, in_keep)
    next(in_rounds)
    in_send, _ = in_rounds.send(None)
    grad_up, mark = weight_back(
        after(me, in_send), up_all[:2], tokens, up_mask, 256, 0, front
    )
    in_send, mark = in_rounds.send(mark)
    grad_up, mark = weight_back(
        after(me, in_send), up_all[2:], tokens, up_mask, 256, front, width, grad_up, [mark]
    )
    grad_in, _ = in_rounds.send(None)
    if cols > 8:
        (layer_out, _), (grad_in, _) = last(out_rounds), last(in_rounds)
    return (layer_out, grad_in, grad_gate, grad_up, grad_down)


def solution(mesh):
    by_row, by_col = P("row", "col"), P("col", "row")
    return jax.shard_map(
        functools.partial(local, mesh.shape["row"], mesh.shape["col"]),
        mesh=mesh,
        in_specs=(by_col, by_col, by_row, by_row, by_col, by_row, by_row, by_col),
        out_specs=(by_col, by_col, by_row, by_row, by_col),
        check_vma=False,
    )
```

```python
import functools

import jax
import jax.numpy as jnp
from jax import lax
from jax.experimental import pallas as pl
from jax.experimental.pallas import tpu as pltpu
from jax.sharding import PartitionSpec as P

BF16 = jnp.bfloat16
F32 = jnp.float32
MIB = 1024 * 1024
NT = (((1,), (1,)), ((), ()))


def dot(a, b):
    return jnp.dot(a, b, preferred_element_type=F32)


def spread(mask, block):
    count = mask.shape[1]
    shape = (count, count * block)
    col = lax.broadcasted_iota(jnp.int32, shape, 1) // block
    row = lax.broadcasted_iota(jnp.int32, shape, 0)
    return dot(mask.astype(BF16), jnp.where(row == col, 1.0, 0.0).astype(BF16))


def masked(w, m, block):
    return jnp.concatenate(
        [
            w[i * block : (i + 1) * block, :]
            * jnp.broadcast_to(m[i : i + 1, :], (block, w.shape[1])).astype(BF16)
            for i in range(w.shape[0] // block)
        ],
        axis=0,
    )


def masked_product(left, right, m, out, block):
    height = left.shape[0]
    some = 256 if height % 256 == 0 else 128
    for top in range(0, height, some):
        got = dot(left[top : top + some, :], right)
        for i in range(some // block):
            line = top // block + i
            out[top + i * block : top + (i + 1) * block, :] = (
                got[i * block : (i + 1) * block, :] * m[line : line + 1, :]
            ).astype(BF16)


def fetches(pairs, columns, size):
    def copy(pair, i):
        source, held, sems = pair
        at = slice(i * size, (i + 1) * size)
        return pltpu.make_async_copy(
            source.at[:, at] if columns else source.at[at, :], held.at[i], sems.at[i]
        )

    def begin():
        for i in range(pairs[0][1].shape[0]):
            for pair in pairs:
                copy(pair, i).start()

    def arrived(i):
        for pair in pairs:
            copy(pair, i).wait()

    return begin, arrived


def at_step(pairs, columns, size, prepare):
    begin, arrived = fetches(pairs, columns, size)
    step = pl.program_id(0)

    @pl.when(step == 0)
    def _():
        begin()
        prepare()

    for i in range(pairs[0][1].shape[0]):
        pl.when(step == i)(functools.partial(arrived, i))
    return step


def spread_steps(mask, block, columns, out):
    full = spread(mask, block)
    steps, height, width = out.shape
    for i in range(steps):
        if columns:
            out[i] = full[:, i * width : (i + 1) * width]
        else:
            out[i] = full[i * height : (i + 1) * height, :]


def order_by_row(me, source, out):
    quarter = out.shape[0] // 4
    for j in range(4):
        at = pl.ds(pl.multiple_of((me ^ j) * quarter, 16), quarter)
        out[j * quarter : (j + 1) * quarter, :] = source[at, :]


def join_halves(me, pieces, out):
    quarter = out.shape[0] // 4
    left = 0
    for x_first, near, far in pieces:
        at = slice(left, left + near.shape[1])
        left += near.shape[1]
        for half, spots in (
            (near, (0, 2) if x_first else (0, 1)),
            (far, (1, 3) if x_first else (2, 3)),
        ):
            for slot, j in enumerate(spots):
                rows = pl.ds(pl.multiple_of((me ^ j) * quarter, 16), quarter)
                out[rows, at] = half[slot * quarter : (slot + 1) * quarter, :]


def put_halves(part, send, keep, at, x_first):
    quarter = part.shape[0] // 4
    kept, sent = ((0, 2), (1, 3)) if x_first else ((0, 1), (2, 3))
    for slot in range(2):
        rows = slice(slot * quarter, (slot + 1) * quarter)
        keep[rows, at] = part[kept[slot] * quarter : (kept[slot] + 1) * quarter, :]
        send[rows, at] = part[sent[slot] * quarter : (sent[slot] + 1) * quarter, :].astype(BF16)


def call(body, name, inputs, kinds, outs, out_kinds, scratch, steps=None, maps=None, aliases={}, macs=500, marks=(), mib=56):
    spec = {
        "s": pl.BlockSpec(memory_space=pltpu.SMEM),
        "v": pl.BlockSpec(memory_space=pltpu.VMEM),
        "h": pl.BlockSpec(memory_space=pl.ANY),
    }
    out_specs = [spec[kind] for kind in out_kinds] if maps is None else maps
    grid = {} if steps is None else {"grid": (steps,)}

    def unmarked(*refs):
        body(*refs[: len(inputs)], *refs[len(inputs) + len(marks) :])

    return pl.pallas_call(
        unmarked,
        in_specs=[spec[kind] for kind in (*kinds, *"h" * len(marks))],
        out_specs=out_specs,
        out_shape=outs,
        scratch_shapes=scratch,
        input_output_aliases=aliases,
        compiler_params=pltpu.CompilerParams(vmem_limit_bytes=mib * MIB),
        cost_estimate=pl.CostEstimate(flops=2 * macs, bytes_accessed=1000, transcendentals=0),
        name=name,
        **grid,
    )(*inputs, *marks)


def tiles_of(count, height, width):
    return [pltpu.VMEM((count, height, width), BF16), pltpu.SemaphoreType.DMA((count,))]


def shaped(*shape, kind=F32):
    return jax.ShapeDtypeStruct(shape, kind)


def parts_of(tile):
    some = min(tile, 256)
    return [slice(left, left + some) for left in range(0, tile, some)]


def forward_part(me, tokens, weight, mask, tile, x_first):
    total, depth = tokens.shape
    width = weight.shape[1]
    steps = width // tile
    block = depth // mask.shape[0]

    def body(me_ref, x_ref, w_hbm, m_ref, send, keep, x_s, m_s, held, sems):
        def prepare():
            order_by_row(me_ref[0], x_ref, x_s)
            spread_steps(m_ref[...], block, True, m_s)

        step = at_step([(w_hbm, held, sems)], True, tile, prepare)
        w, m = held.at[step], m_s[step]
        for at in parts_of(tile):
            part = dot(x_s[...], masked(w.at[:, at], m[:, at], block))
            put_halves(part, send, keep, at, x_first)

    return call(
        body,
        "forward_part",
        (me, tokens, weight, mask),
        "svhv",
        [shaped(total // 2, width, kind=BF16), shaped(total // 2, width)],
        None,
        [
            pltpu.VMEM((total, depth), BF16),
            pltpu.VMEM((steps, mask.shape[0], tile), F32),
            *tiles_of(steps, depth, tile),
        ],
        steps,
        [pl.BlockSpec((total // 2, tile), lambda i: (0, i))] * 2,
        mib=32,
    )


def hidden_part(me, grads, weight, mask, tile):
    total, depth = grads.shape
    steps = weight.shape[0] // tile
    front = (steps + 1) // 2
    block = depth // mask.shape[1]
    per = tile // block

    def body(me_ref, x_ref, w_hbm, m_ref, a_send, a_keep, b_send, b_keep, x_s, m_s, held, sems):
        def prepare():
            order_by_row(me_ref[0], x_ref, x_s)
            spread_steps(m_ref[...], block, False, m_s)

        step = at_step([(w_hbm, held, sems)], False, tile, prepare)
        w, m = held.at[step], m_s[step]

        def put(send, keep, x_first):
            for at in parts_of(tile):
                rows = slice(at.start // block, at.stop // block)
                part = lax.dot_general(
                    x_s[...], masked(w.at[at, :], m[rows, :], block), NT, preferred_element_type=F32
                )
                put_halves(part, send, keep, at, x_first)

        pl.when(step < front)(functools.partial(put, a_send, a_keep, True))
        pl.when(step >= front)(functools.partial(put, b_send, b_keep, False))

    return call(
        body,
        "hidden_part",
        (me, grads, weight, mask),
        "svhv",
        [
            shaped(total // 2, count * tile, kind=kind)
            for count in (front, steps - front)
            for kind in (BF16, F32)
        ],
        None,
        [
            pltpu.VMEM((total, depth), BF16),
            pltpu.VMEM((steps, per, depth), F32),
            *tiles_of(steps, tile, depth),
        ],
        steps,
        [pl.BlockSpec((total // 2, tile), lambda i: (0, jnp.minimum(i, front - 1)))] * 2
        + [pl.BlockSpec((total // 2, tile), lambda i: (0, jnp.maximum(i - front, 0)))] * 2,
        mib=32,
    )


def down_back(me, pieces, grads, weight, mask, tile):
    total, depth = grads.shape
    width = weight.shape[0]
    block = width // mask.shape[0]
    steps, slots = depth // tile, 4

    def body(me_ref, h0, h1, h2, h3, g_ref, w_hbm, m_ref, gw, send, keep, hid, hid_t, held, sems, stage, outs):
        begin, arrived = fetches([(w_hbm, held, sems)], True, tile)
        begin()
        join_halves(me_ref[0], ((True, h0, h1), (False, h2, h3)), hid)
        hid_t[...] = hid[...].T
        m = spread(m_ref[...], block)

        def leave(i):
            at = slice(i * tile, (i + 1) * tile)
            return pltpu.make_async_copy(stage.at[i % slots], gw.at[:, at], outs.at[i % slots])

        arrived(0)
        w = masked(held.at[0], m[:, :tile], block)
        for i in range(steps):
            at = slice(i * tile, (i + 1) * tile)
            now = w
            if i >= slots:
                leave(i - slots).wait()
            if i + 1 < steps:
                arrived(i + 1)
                w = masked(held.at[i + 1], m[:, (i + 1) * tile : (i + 2) * tile], block)
            out = dot(hid[...], now)
            keep[:, at] = out[: total // 2, :]
            send[:, at] = out[total // 2 :, :]
            masked_product(hid_t, g_ref[:, at], m[:, at], stage.at[i % slots], block)
            leave(i).start()
        for i in range(max(steps - slots, 0), steps):
            leave(i).wait()

    return call(
        body,
        "down_back",
        (me, *pieces, grads, weight, mask),
        "svvvvvhv",
        [shaped(width, depth, kind=BF16), shaped(total // 2, depth), shaped(total // 2, depth)],
        "hvv",
        [
            pltpu.VMEM((total, width), BF16),
            pltpu.VMEM((width, total), BF16),
            *tiles_of(steps, width, tile),
            pltpu.VMEM((slots, width, tile), BF16),
            pltpu.SemaphoreType.DMA((slots,)),
        ],
        macs=2 * total * depth * width,
        mib=44,
    )


def input_back(me, gate_pieces, up_pieces, gate_w, up_w, gate_m, up_m, tile, marks=()):
    depth, width = gate_w.shape
    total = 2 * gate_pieces[0].shape[0]
    block = depth // gate_m.shape[0]
    steps, per = depth // tile, tile // block

    def body(me_ref, *refs):
        pieces, (gw, uw, gm, um, send, keep, a_s, b_s, gm_s, um_s, gh, gs, uh, us) = refs[:8], refs[8:]

        def prepare():
            join_halves(me_ref[0], ((True, *pieces[0:2]), (False, *pieces[2:4])), a_s)
            join_halves(me_ref[0], ((True, *pieces[4:6]), (False, *pieces[6:8])), b_s)
            spread_steps(gm[...], block, False, gm_s)
            spread_steps(um[...], block, False, um_s)

        step = at_step([(gw, gh, gs), (uw, uh, us)], False, tile, prepare)
        out = lax.dot_general(
            a_s[...], masked(gh.at[step], gm_s[step], block), NT, preferred_element_type=F32
        )
        out += lax.dot_general(
            b_s[...], masked(uh.at[step], um_s[step], block), NT, preferred_element_type=F32
        )
        keep[...] = out[: total // 2, :]
        send[...] = out[total // 2 :, :]

    return call(
        body,
        "input_back",
        (me, *gate_pieces, *up_pieces, gate_w, up_w, gate_m, up_m),
        "s" + "v" * 8 + "hhvv",
        [shaped(total // 2, depth), shaped(total // 2, depth)],
        None,
        [
            pltpu.VMEM((total, width), BF16),
            pltpu.VMEM((total, width), BF16),
            pltpu.VMEM((steps, per, width), F32),
            pltpu.VMEM((steps, per, width), F32),
            *tiles_of(steps, tile, width),
            *tiles_of(steps, tile, width),
        ],
        steps,
        [pl.BlockSpec((total // 2, tile), lambda i: (0, i))] * 2,
        macs=2 * total * depth * width,
        marks=marks,
        mib=50,
    )


def weight_back(me, pieces, tokens, mask, tile, left, right, earlier=None, marks=()):
    total, depth = tokens.shape
    block = depth // mask.shape[0]
    width = mask.shape[1] * block
    steps, slots = depth // tile, 6
    known = [] if earlier is None else [earlier]

    def body(me_ref, x_ref, m_ref, *refs):
        refs, (out, mark, a_s, stage, sems) = refs[:-5], refs[-5:]
        mark[...] = jnp.zeros_like(mark)

        def leave(i):
            rows = slice(i * tile, (i + 1) * tile)
            return pltpu.make_async_copy(
                stage.at[i % slots], out.at[rows, left:right], sems.at[i % slots]
            )

        ways = (True, False) if left == 0 else (False,)
        join_halves(
            me_ref[0],
            [(way, *refs[2 * n : 2 * n + 2]) for n, way in enumerate(ways[: len(pieces) // 2])],
            a_s,
        )
        m = spread(m_ref[...], block)[:, left:right]
        for i in range(steps):
            if i >= slots:
                leave(i - slots).wait()
            got = lax.dot_general(
                x_ref[:, i * tile : (i + 1) * tile],
                a_s[...],
                (((0,), (0,)), ((), ())),
                preferred_element_type=F32,
            )
            for j in range(tile // block):
                line = i * (tile // block) + j
                stage[i % slots, j * block : (j + 1) * block, :] = (
                    got[j * block : (j + 1) * block, :] * m[line : line + 1, :]
                ).astype(BF16)
            leave(i).start()
        for i in range(max(steps - slots, 0), steps):
            leave(i).wait()

    return call(
        body,
        "weight_back",
        (me, tokens, mask, *pieces, *known),
        "svv" + "v" * len(pieces) + "h" * len(known),
        [shaped(depth, width, kind=BF16), shaped(8, 128)],
        "hv",
        [pltpu.VMEM((total, right - left), BF16), *tiles_of(slots, tile, right - left)],
        aliases={3 + len(pieces): 0} if known else {},
        macs=total * depth * (right - left),
        marks=marks,
        mib=26,
    )


def swap(value, axis, size, bit):
    return lax.ppermute(value, axis, [(i, i ^ bit) for i in range(size)])


def after(value, *earlier):
    return lax.optimization_barrier((value, *earlier))[0]


def local(rows, cols, tokens_in, grad_out, gate_w, up_w, down_w, gate_mask, up_mask, down_mask):
    me = lax.axis_index("row").astype(jnp.int32)[None]
    width = gate_w.shape[1]
    wide = 512 if width % 512 == 0 else 128

    def over_row(value, bit):
        return swap(value, "row", rows, bit)

    def over_col(value, bit):
        return swap(value, "col", cols, bit)

    def halve(total):
        half = total.shape[0] // 2
        return total[:half], total[half:].astype(BF16)

    def gathering(own):
        bit = cols // 2
        while bit:
            got = over_col(own, bit)
            earlier = yield own
            got = got if earlier is None else after(got, earlier)
            own = jnp.concatenate([own, got], axis=0)
            bit //= 2
        yield own

    def leaving(send, keep):
        bit, earlier = 1, None
        while bit < cols:
            got = over_col(send, bit)
            earlier = yield send, earlier
            if earlier is not None:
                got, earlier = lax.optimization_barrier((got, earlier))
            keep = keep + got
            bit *= 2
            if bit < cols:
                keep, send = halve(keep)
        yield keep.astype(BF16), earlier

    def last(rounds):
        for value in rounds:
            pass
        return value

    rounds = gathering(tokens_in)
    near = tokens = next(rounds)
    for value in rounds:
        near, tokens = tokens, value
    rounds = gathering(after(grad_out, near))
    next(rounds)
    gate_send, gate_keep = forward_part(me, tokens, gate_w, gate_mask, wide, True)
    gate_got = over_row(gate_send, 1)
    rounds.send(gate_send)
    up_send, up_keep = forward_part(after(me, gate_send), tokens, up_w, up_mask, wide, False)
    up_got = over_row(up_send, 2)
    rounds.send(up_send)
    grads = last(rounds)
    a_send, a_keep, b_send, b_keep = hidden_part(
        after(me, up_send), grads, down_w, after(down_mask, gate_send), wide
    )
    a_got, b_got = over_row(a_send, 1), over_row(b_send, 2)
    gate_got, up_got, a_send = lax.optimization_barrier((gate_got, up_got, a_send))
    gate_keep, gate_send = halve(gate_keep + gate_got)
    up_keep, up_send = halve(up_keep + up_got)
    gate_got, up_got = over_row(gate_send, 2), over_row(up_send, 1)

    def near_halves(front, rest, *earlier):
        front, rest = lax.optimization_barrier((front, rest, *earlier))[:2]
        return front, over_row(front, 2), rest, over_row(rest, 1)

    def all_halves(front, front_got, rest, rest_got, *earlier):
        front_got, rest_got = lax.optimization_barrier((front_got, rest_got, *earlier))[:2]
        front = jnp.concatenate([front, front_got], axis=0)
        rest = jnp.concatenate([rest, rest_got], axis=0)
        return front, over_row(front, 1), rest, over_row(rest, 2)

    front = a_keep.shape[1]
    gate_pre, up_pre = gate_keep + gate_got, up_keep + up_got
    hidden = (jax.nn.sigmoid(gate_pre) * gate_pre * up_pre).astype(BF16)
    hidden_a, hidden_b, gate_pre, up_pre = lax.optimization_barrier(
        (hidden[:, :front], hidden[:, front:], gate_pre, up_pre)
    )
    hidden_all = all_halves(*near_halves(hidden_a, hidden_b))

    a_keep, a_send = halve(a_keep + after(a_got, gate_send, up_send))
    b_keep, b_send = halve(b_keep + after(b_got, gate_send, up_send))
    a_got, b_got = over_row(a_send, 2), over_row(b_send, 1)
    a_got, b_got = after(a_got, hidden_a), after(b_got, hidden_a)
    pre = []
    for at, grad_hidden in ((slice(None, front), a_keep + a_got), (slice(front, None), b_keep + b_got)):
        gate, up = gate_pre[:, at], up_pre[:, at]
        sig = jax.nn.sigmoid(gate)
        pre.append((grad_hidden * up * sig * (1.0 + gate * (1.0 - sig))).astype(BF16))
        pre.append((grad_hidden * (gate * sig)).astype(BF16))
    gate_near = near_halves(pre[0], pre[2], hidden_all[0], hidden_all[2])
    gate_all = all_halves(*gate_near, hidden_all[1], hidden_all[3])
    up_near = near_halves(pre[1], pre[3], gate_all[0], gate_all[2])
    grad_down, out_send, out_keep = down_back(
        after(me, gate_all[0], gate_all[2]), hidden_all, grads, down_w, down_mask, 256
    )
    up_near = list(up_near)
    up_near[1], up_near[3], out_send = lax.optimization_barrier((up_near[1], up_near[3], out_send))
    up_all = all_halves(*up_near)
    out_rounds = leaving(out_send, out_keep)
    next(out_rounds)
    grad_gate, mark = weight_back(
        after(me, out_send), gate_all[:2], tokens, gate_mask, 256, 0, front
    )
    _, mark = out_rounds.send(mark)
    grad_gate, mark = weight_back(
        me, gate_all[2:], tokens, gate_mask, 256, front, width, grad_gate, [mark]
    )
    _, mark = out_rounds.send(mark)
    in_send, in_keep = input_back(
        me, gate_all, up_all, gate_w, up_w, gate_mask, up_mask, 256, [mark]
    )
    layer_out, in_send = out_rounds.send(in_send)
    in_rounds = leaving(in_send, in_keep)
    next(in_rounds)
    in_send, _ = in_rounds.send(None)
    grad_up, mark = weight_back(
        after(me, in_send), up_all[:2], tokens, up_mask, 256, 0, front
    )
    in_send, mark = in_rounds.send(mark)
    grad_up, mark = weight_back(
        after(me, in_send), up_all[2:], tokens, up_mask, 256, front, width, grad_up, [mark]
    )
    grad_in, _ = in_rounds.send(None)
    if cols > 8:
        (layer_out, _), (grad_in, _) = last(out_rounds), last(in_rounds)
    return (layer_out, grad_in, grad_gate, grad_up, grad_down)


def solution(mesh):
    by_row, by_col = P("row", "col"), P("col", "row")
    return jax.shard_map(
        functools.partial(local, mesh.shape["row"], mesh.shape["col"]),
        mesh=mesh,
        in_specs=(by_col, by_col, by_row, by_row, by_col, by_row, by_row, by_col),
        out_specs=(by_col, by_col, by_row, by_row, by_col),
        check_vma=False,
    )
```

```python
import functools

import jax
import jax.numpy as jnp
from jax import lax
from jax.experimental import pallas as pl
from jax.experimental.pallas import tpu as pltpu
from jax.sharding import PartitionSpec as P

BF16 = jnp.bfloat16
F32 = jnp.float32
MIB = 1024 * 1024
NT = (((1,), (1,)), ((), ()))


def dot(a, b):
    return jnp.dot(a, b, preferred_element_type=F32)


def spread(mask, block):
    count = mask.shape[1]
    shape = (count, count * block)
    col = lax.broadcasted_iota(jnp.int32, shape, 1) // block
    row = lax.broadcasted_iota(jnp.int32, shape, 0)
    return dot(mask.astype(BF16), jnp.where(row == col, 1.0, 0.0).astype(BF16))


def masked(w, m, block):
    return jnp.concatenate(
        [
            w[i * block : (i + 1) * block, :]
            * jnp.broadcast_to(m[i : i + 1, :], (block, w.shape[1])).astype(BF16)
            for i in range(w.shape[0] // block)
        ],
        axis=0,
    )


def masked_product(left, right, m, out, block):
    height = left.shape[0]
    some = 256 if height % 256 == 0 else 128
    for top in range(0, height, some):
        got = dot(left[top : top + some, :], right)
        for i in range(some // block):
            line = top // block + i
            out[top + i * block : top + (i + 1) * block, :] = (
                got[i * block : (i + 1) * block, :] * m[line : line + 1, :]
            ).astype(BF16)


def fetches(pairs, columns, size):
    def copy(pair, i):
        source, held, sems = pair
        at = slice(i * size, (i + 1) * size)
        return pltpu.make_async_copy(
            source.at[:, at] if columns else source.at[at, :], held.at[i], sems.at[i]
        )

    def begin():
        for i in range(pairs[0][1].shape[0]):
            for pair in pairs:
                copy(pair, i).start()

    def arrived(i):
        for pair in pairs:
            copy(pair, i).wait()

    return begin, arrived


def at_step(pairs, columns, size, prepare):
    begin, arrived = fetches(pairs, columns, size)
    step = pl.program_id(0)

    @pl.when(step == 0)
    def _():
        begin()
        prepare()

    for i in range(pairs[0][1].shape[0]):
        pl.when(step == i)(functools.partial(arrived, i))
    return step


def spread_steps(mask, block, columns, out):
    full = spread(mask, block)
    steps, height, width = out.shape
    for i in range(steps):
        if columns:
            out[i] = full[:, i * width : (i + 1) * width]
        else:
            out[i] = full[i * height : (i + 1) * height, :]


def order_by_row(me, source, out):
    quarter = out.shape[0] // 4
    for j in range(4):
        at = pl.ds(pl.multiple_of((me ^ j) * quarter, 16), quarter)
        out[j * quarter : (j + 1) * quarter, :] = source[at, :]


def join_halves(me, pieces, out):
    quarter = out.shape[0] // 4
    left = 0
    for x_first, near, far in pieces:
        at = slice(left, left + near.shape[1])
        left += near.shape[1]
        for half, spots in (
            (near, (0, 2) if x_first else (0, 1)),
            (far, (1, 3) if x_first else (2, 3)),
        ):
            for slot, j in enumerate(spots):
                rows = pl.ds(pl.multiple_of((me ^ j) * quarter, 16), quarter)
                out[rows, at] = half[slot * quarter : (slot + 1) * quarter, :]


def put_halves(part, send, keep, at, x_first):
    quarter = part.shape[0] // 4
    kept, sent = ((0, 2), (1, 3)) if x_first else ((0, 1), (2, 3))
    for slot in range(2):
        rows = slice(slot * quarter, (slot + 1) * quarter)
        keep[rows, at] = part[kept[slot] * quarter : (kept[slot] + 1) * quarter, :]
        send[rows, at] = part[sent[slot] * quarter : (sent[slot] + 1) * quarter, :].astype(BF16)


def call(body, name, inputs, kinds, outs, out_kinds, scratch, steps=None, maps=None, aliases={}, macs=500, marks=(), mib=56):
    spec = {
        "s": pl.BlockSpec(memory_space=pltpu.SMEM),
        "v": pl.BlockSpec(memory_space=pltpu.VMEM),
        "h": pl.BlockSpec(memory_space=pl.ANY),
    }
    out_specs = [spec[kind] for kind in out_kinds] if maps is None else maps
    grid = {} if steps is None else {"grid": (steps,)}

    def unmarked(*refs):
        body(*refs[: len(inputs)], *refs[len(inputs) + len(marks) :])

    return pl.pallas_call(
        unmarked,
        in_specs=[spec[kind] for kind in (*kinds, *"h" * len(marks))],
        out_specs=out_specs,
        out_shape=outs,
        scratch_shapes=scratch,
        input_output_aliases=aliases,
        compiler_params=pltpu.CompilerParams(vmem_limit_bytes=mib * MIB),
        cost_estimate=pl.CostEstimate(flops=2 * macs, bytes_accessed=1000, transcendentals=0),
        name=name,
        **grid,
    )(*inputs, *marks)


def tiles_of(count, height, width):
    return [pltpu.VMEM((count, height, width), BF16), pltpu.SemaphoreType.DMA((count,))]


def shaped(*shape, kind=F32):
    return jax.ShapeDtypeStruct(shape, kind)


def parts_of(tile):
    some = min(tile, 256)
    return [slice(left, left + some) for left in range(0, tile, some)]


def forward_part(me, tokens, weight, mask, tile, x_first):
    total, depth = tokens.shape
    width = weight.shape[1]
    steps = width // tile
    block = depth // mask.shape[0]

    def body(me_ref, x_ref, w_hbm, m_ref, send, keep, x_s, m_s, held, sems):
        def prepare():
            order_by_row(me_ref[0], x_ref, x_s)
            spread_steps(m_ref[...], block, True, m_s)

        step = at_step([(w_hbm, held, sems)], True, tile, prepare)
        w, m = held.at[step], m_s[step]
        for at in parts_of(tile):
            part = dot(x_s[...], masked(w.at[:, at], m[:, at], block))
            put_halves(part, send, keep, at, x_first)

    return call(
        body,
        "forward_part",
        (me, tokens, weight, mask),
        "svhv",
        [shaped(total // 2, width, kind=BF16), shaped(total // 2, width)],
        None,
        [
            pltpu.VMEM((total, depth), BF16),
            pltpu.VMEM((steps, mask.shape[0], tile), F32),
            *tiles_of(steps, depth, tile),
        ],
        steps,
        [pl.BlockSpec((total // 2, tile), lambda i: (0, i))] * 2,
        mib=51,
    )


def hidden_part(me, grads, weight, mask, tile):
    total, depth = grads.shape
    steps = weight.shape[0] // tile
    front = (steps + 1) // 2
    block = depth // mask.shape[1]
    per = tile // block

    def body(me_ref, x_ref, w_hbm, m_ref, a_send, a_keep, b_send, b_keep, x_s, m_s, held, sems):
        def prepare():
            order_by_row(me_ref[0], x_ref, x_s)
            spread_steps(m_ref[...], block, False, m_s)

        step = at_step([(w_hbm, held, sems)], False, tile, prepare)
        w, m = held.at[step], m_s[step]

        def put(send, keep, x_first):
            for at in parts_of(tile):
                rows = slice(at.start // block, at.stop // block)
                part = lax.dot_general(
                    x_s[...], masked(w.at[at, :], m[rows, :], block), NT, preferred_element_type=F32
                )
                put_halves(part, send, keep, at, x_first)

        pl.when(step < front)(functools.partial(put, a_send, a_keep, True))
        pl.when(step >= front)(functools.partial(put, b_send, b_keep, False))

    return call(
        body,
        "hidden_part",
        (me, grads, weight, mask),
        "svhv",
        [
            shaped(total // 2, count * tile, kind=kind)
            for count in (front, steps - front)
            for kind in (BF16, F32)
        ],
        None,
        [
            pltpu.VMEM((total, depth), BF16),
            pltpu.VMEM((steps, per, depth), F32),
            *tiles_of(steps, tile, depth),
        ],
        steps,
        [pl.BlockSpec((total // 2, tile), lambda i: (0, jnp.minimum(i, front - 1)))] * 2
        + [pl.BlockSpec((total // 2, tile), lambda i: (0, jnp.maximum(i - front, 0)))] * 2,
        mib=51,
    )


def down_back(me, pieces, grads, weight, mask, tile):
    total, depth = grads.shape
    width = weight.shape[0]
    block = width // mask.shape[0]
    steps, slots = depth // tile, 4

    def body(me_ref, h0, h1, h2, h3, g_ref, w_hbm, m_ref, gw, send, keep, hid, hid_t, held, sems, stage, outs):
        begin, arrived = fetches([(w_hbm, held, sems)], True, tile)
        begin()
        join_halves(me_ref[0], ((True, h0, h1), (False, h2, h3)), hid)
        hid_t[...] = hid[...].T
        m = spread(m_ref[...], block)

        def leave(i):
            at = slice(i * tile, (i + 1) * tile)
            return pltpu.make_async_copy(stage.at[i % slots], gw.at[:, at], outs.at[i % slots])

        arrived(0)
        w = masked(held.at[0], m[:, :tile], block)
        for i in range(steps):
            at = slice(i * tile, (i + 1) * tile)
            now = w
            if i >= slots:
                leave(i - slots).wait()
            if i + 1 < steps:
                arrived(i + 1)
                w = masked(held.at[i + 1], m[:, (i + 1) * tile : (i + 2) * tile], block)
            out = dot(hid[...], now)
            keep[:, at] = out[: total // 2, :]
            send[:, at] = out[total // 2 :, :]
            masked_product(hid_t, g_ref[:, at], m[:, at], stage.at[i % slots], block)
            leave(i).start()
        for i in range(max(steps - slots, 0), steps):
            leave(i).wait()

    return call(
        body,
        "down_back",
        (me, *pieces, grads, weight, mask),
        "svvvvvhv",
        [shaped(width, depth, kind=BF16), shaped(total // 2, depth), shaped(total // 2, depth)],
        "hvv",
        [
            pltpu.VMEM((total, width), BF16),
            pltpu.VMEM((width, total), BF16),
            *tiles_of(steps, width, tile),
            pltpu.VMEM((slots, width, tile), BF16),
            pltpu.SemaphoreType.DMA((slots,)),
        ],
        macs=2 * total * depth * width,
        mib=44,
    )


def input_back(me, gate_pieces, up_pieces, gate_w, up_w, gate_m, up_m, tile, marks=()):
    depth, width = gate_w.shape
    total = 2 * gate_pieces[0].shape[0]
    block = depth // gate_m.shape[0]
    steps, per = depth // tile, tile // block

    def body(me_ref, *refs):
        pieces, (gw, uw, gm, um, send, keep, a_s, b_s, gm_s, um_s, gh, gs, uh, us) = refs[:8], refs[8:]

        def prepare():
            join_halves(me_ref[0], ((True, *pieces[0:2]), (False, *pieces[2:4])), a_s)
            join_halves(me_ref[0], ((True, *pieces[4:6]), (False, *pieces[6:8])), b_s)
            spread_steps(gm[...], block, False, gm_s)
            spread_steps(um[...], block, False, um_s)

        step = at_step([(gw, gh, gs), (uw, uh, us)], False, tile, prepare)
        out = lax.dot_general(
            a_s[...], masked(gh.at[step], gm_s[step], block), NT, preferred_element_type=F32
        )
        out += lax.dot_general(
            b_s[...], masked(uh.at[step], um_s[step], block), NT, preferred_element_type=F32
        )
        keep[...] = out[: total // 2, :]
        send[...] = out[total // 2 :, :]

    return call(
        body,
        "input_back",
        (me, *gate_pieces, *up_pieces, gate_w, up_w, gate_m, up_m),
        "s" + "v" * 8 + "hhvv",
        [shaped(total // 2, depth), shaped(total // 2, depth)],
        None,
        [
            pltpu.VMEM((total, width), BF16),
            pltpu.VMEM((total, width), BF16),
            pltpu.VMEM((steps, per, width), F32),
            pltpu.VMEM((steps, per, width), F32),
            *tiles_of(steps, tile, width),
            *tiles_of(steps, tile, width),
        ],
        steps,
        [pl.BlockSpec((total // 2, tile), lambda i: (0, i))] * 2,
        macs=2 * total * depth * width,
        marks=marks,
        mib=50,
    )


def weight_back(me, pieces, tokens, mask, tile, left, right, earlier=None, marks=()):
    total, depth = tokens.shape
    block = depth // mask.shape[0]
    width = mask.shape[1] * block
    steps, slots = depth // tile, 6
    known = [] if earlier is None else [earlier]

    def body(me_ref, x_ref, m_ref, *refs):
        refs, (out, mark, a_s, stage, sems) = refs[:-5], refs[-5:]
        mark[...] = jnp.zeros_like(mark)

        def leave(i):
            rows = slice(i * tile, (i + 1) * tile)
            return pltpu.make_async_copy(
                stage.at[i % slots], out.at[rows, left:right], sems.at[i % slots]
            )

        ways = (True, False) if left == 0 else (False,)
        join_halves(
            me_ref[0],
            [(way, *refs[2 * n : 2 * n + 2]) for n, way in enumerate(ways[: len(pieces) // 2])],
            a_s,
        )
        m = spread(m_ref[...], block)[:, left:right]
        for i in range(steps):
            if i >= slots:
                leave(i - slots).wait()
            got = lax.dot_general(
                x_ref[:, i * tile : (i + 1) * tile],
                a_s[...],
                (((0,), (0,)), ((), ())),
                preferred_element_type=F32,
            )
            for j in range(tile // block):
                line = i * (tile // block) + j
                stage[i % slots, j * block : (j + 1) * block, :] = (
                    got[j * block : (j + 1) * block, :] * m[line : line + 1, :]
                ).astype(BF16)
            leave(i).start()
        for i in range(max(steps - slots, 0), steps):
            leave(i).wait()

    return call(
        body,
        "weight_back",
        (me, tokens, mask, *pieces, *known),
        "svv" + "v" * len(pieces) + "h" * len(known),
        [shaped(depth, width, kind=BF16), shaped(8, 128)],
        "hv",
        [pltpu.VMEM((total, right - left), BF16), *tiles_of(slots, tile, right - left)],
        aliases={3 + len(pieces): 0} if known else {},
        macs=total * depth * (right - left),
        marks=marks,
        mib=26,
    )


def swap(value, axis, size, bit):
    return lax.ppermute(value, axis, [(i, i ^ bit) for i in range(size)])


def after(value, *earlier):
    return lax.optimization_barrier((value, *earlier))[0]


def local(rows, cols, tokens_in, grad_out, gate_w, up_w, down_w, gate_mask, up_mask, down_mask):
    me = lax.axis_index("row").astype(jnp.int32)[None]
    width = gate_w.shape[1]
    wide = 512 if width % 512 == 0 else 128

    def over_row(value, bit):
        return swap(value, "row", rows, bit)

    def over_col(value, bit):
        return swap(value, "col", cols, bit)

    def halve(total):
        half = total.shape[0] // 2
        return total[:half], total[half:].astype(BF16)

    def gathering(own):
        bit = cols // 2
        while bit:
            got = over_col(own, bit)
            earlier = yield own
            got = got if earlier is None else after(got, earlier)
            own = jnp.concatenate([own, got], axis=0)
            bit //= 2
        yield own

    def leaving(send, keep):
        bit, earlier = 1, None
        while bit < cols:
            got = over_col(send, bit)
            earlier = yield send, earlier
            if earlier is not None:
                got, earlier = lax.optimization_barrier((got, earlier))
            keep = keep + got
            bit *= 2
            if bit < cols:
                keep, send = halve(keep)
        yield keep.astype(BF16), earlier

    def last(rounds):
        for value in rounds:
            pass
        return value

    rounds = gathering(tokens_in)
    near = tokens = next(rounds)
    for value in rounds:
        near, tokens = tokens, value
    rounds = gathering(after(grad_out, near))
    next(rounds)
    gate_send, gate_keep = forward_part(me, tokens, gate_w, gate_mask, wide, True)
    gate_got = over_row(gate_send, 1)
    rounds.send(gate_send)
    up_send, up_keep = forward_part(after(me, gate_send), tokens, up_w, up_mask, wide, False)
    up_got = over_row(up_send, 2)
    rounds.send(up_send)
    grads = last(rounds)
    a_send, a_keep, b_send, b_keep = hidden_part(
        after(me, up_send), grads, down_w, after(down_mask, gate_send), wide
    )
    a_got, b_got = over_row(a_send, 1), over_row(b_send, 2)
    gate_got, up_got, a_send = lax.optimization_barrier((gate_got, up_got, a_send))
    gate_keep, gate_send = halve(gate_keep + gate_got)
    up_keep, up_send = halve(up_keep + up_got)
    gate_got, up_got = over_row(gate_send, 2), over_row(up_send, 1)

    def near_halves(front, rest, *earlier):
        front, rest = lax.optimization_barrier((front, rest, *earlier))[:2]
        return front, over_row(front, 2), rest, over_row(rest, 1)

    def all_halves(front, front_got, rest, rest_got, *earlier):
        front_got, rest_got = lax.optimization_barrier((front_got, rest_got, *earlier))[:2]
        front = jnp.concatenate([front, front_got], axis=0)
        rest = jnp.concatenate([rest, rest_got], axis=0)
        return front, over_row(front, 1), rest, over_row(rest, 2)

    front = a_keep.shape[1]
    gate_pre, up_pre = gate_keep + gate_got, up_keep + up_got
    hidden = (jax.nn.sigmoid(gate_pre) * gate_pre * up_pre).astype(BF16)
    hidden_a, hidden_b, gate_pre, up_pre = lax.optimization_barrier(
        (hidden[:, :front], hidden[:, front:], gate_pre, up_pre)
    )
    hidden_all = all_halves(*near_halves(hidden_a, hidden_b))

    a_keep, a_send = halve(a_keep + after(a_got, gate_send, up_send))
    b_keep, b_send = halve(b_keep + after(b_got, gate_send, up_send))
    a_got, b_got = over_row(a_send, 2), over_row(b_send, 1)
    a_got, b_got = after(a_got, hidden_a), after(b_got, hidden_a)
    pre = []
    for at, grad_hidden in ((slice(None, front), a_keep + a_got), (slice(front, None), b_keep + b_got)):
        gate, up = gate_pre[:, at], up_pre[:, at]
        sig = jax.nn.sigmoid(gate)
        pre.append((grad_hidden * up * sig * (1.0 + gate * (1.0 - sig))).astype(BF16))
        pre.append((grad_hidden * (gate * sig)).astype(BF16))
    gate_near = near_halves(pre[0], pre[2], hidden_all[0], hidden_all[2])
    gate_all = all_halves(*gate_near, hidden_all[1], hidden_all[3])
    up_near = near_halves(pre[1], pre[3], gate_all[0], gate_all[2])
    grad_down, out_send, out_keep = down_back(
        after(me, gate_all[0], gate_all[2]), hidden_all, grads, down_w, down_mask, 256
    )
    up_near = list(up_near)
    up_near[1], up_near[3], out_send = lax.optimization_barrier((up_near[1], up_near[3], out_send))
    up_all = all_halves(*up_near)
    out_rounds = leaving(out_send, out_keep)
    next(out_rounds)
    grad_gate, mark = weight_back(
        after(me, out_send), gate_all[:2], tokens, gate_mask, 256, 0, front
    )
    _, mark = out_rounds.send(mark)
    grad_gate, mark = weight_back(
        me, gate_all[2:], tokens, gate_mask, 256, front, width, grad_gate, [mark]
    )
    _, mark = out_rounds.send(mark)
    in_send, in_keep = input_back(
        me, gate_all, up_all, gate_w, up_w, gate_mask, up_mask, 256, [mark]
    )
    layer_out, in_send = out_rounds.send(in_send)
    in_rounds = leaving(in_send, in_keep)
    next(in_rounds)
    in_send, _ = in_rounds.send(None)
    grad_up, mark = weight_back(
        after(me, in_send), up_all[:2], tokens, up_mask, 256, 0, front
    )
    in_send, mark = in_rounds.send(mark)
    grad_up, mark = weight_back(
        after(me, in_send), up_all[2:], tokens, up_mask, 256, front, width, grad_up, [mark]
    )
    grad_in, _ = in_rounds.send(None)
    if cols > 8:
        (layer_out, _), (grad_in, _) = last(out_rounds), last(in_rounds)
    return (layer_out, grad_in, grad_gate, grad_up, grad_down)


def solution(mesh):
    by_row, by_col = P("row", "col"), P("col", "row")
    return jax.shard_map(
        functools.partial(local, mesh.shape["row"], mesh.shape["col"]),
        mesh=mesh,
        in_specs=(by_col, by_col, by_row, by_row, by_col, by_row, by_row, by_col),
        out_specs=(by_col, by_col, by_row, by_row, by_col),
        check_vma=False,
    )
```
